32 devices in a mesh: req: 4 (over y, core), seq: 8 (over z, x).
Axes of the slice: x: 2, y: 2, z: 4, core: 2. Of those that a mesh axis runs over, the one named last changes fastest.
Arguments:
- embedded: bfloat16 [4, 48, 3584], P(None, 'req'), may hold values from -6 to 6
- cache_keys: bfloat16 [4, 4096, 2048], P('req', 'seq'), may hold values from -6 to 6
- cache_values: bfloat16 [4, 4096, 2048], P('req', 'seq'), may hold values from -6 to 6
- token_owner: int32 [4, 4096], P('req', 'seq'), may hold values from 0 to 11, as said below
- dealing: int32 [48], replicated, may hold values from 0 to 47, as said below
- lengths: int32 [48], replicated, may hold values from 1 to 2048, as said below
- project_weight: bfloat16 [3584, 8192], P(None, 'seq')
- output_weight: bfloat16 [4096, 3584], P('seq'), may hold values from -0.09375 to 0.09375
- gate_weight: bfloat16 [3584, 14336], P(None, ('req', 'seq')), may hold values from -0.09375 to 0.09375
- up_weight: bfloat16 [3584, 14336], P(None, ('req', 'seq')), may hold values from -0.09375 to 0.09375
- down_weight: bfloat16 [14336, 3584], P(('req', 'seq')), may hold values from -0.046875 to 0.046875
- gain_first: float32 [3584], replicated, may hold values from 0.1 to 1.9
- gain_second: float32 [3584], replicated, may hold values from 0.1 to 1.9
- gain_third: float32 [3584], replicated, may hold values from 0.1 to 1.9
- gain_fourth: float32 [3584], replicated, may hold values from 0.1 to 1.9
Outputs:
- results: bfloat16 [4, 48, 3584], P(None, 'req')
The draws below stay inside these ranges and needn't reach their ends.
Inputs may be any that keep to these rules, and one draw needn't show every extreme that they name: A permutation of the requests; slot i of req group g serves request dealing[g * 12 + i]. The lengths of the 12 requests dealt to one group sum to 4096; in every group the longest is exactly 2048. `token_owner`: each slot owns a contiguous run of its group's pool, runs in slot order, as many tokens as its request's length.
All inputs are finite; a program needn't handle non-finite values.
Results may differ from the reference program's by a relative error of at most 0.012.
The reference program's roundings to bfloat16 on the way count: a program that leaves them out, or rounds other values in their place, can miss the bound.
Values may be sent and summed in bfloat16 or wider, within the bound.
A program may use at most 128 MiB of HBM per device.

```python
import math
import jax
import jax.numpy as jnp
from jax import lax

D = 3584
H = 16
KVH = 8
HD = 256
FF = 14336
REQ_DEV = 12
STEPS = 4
R = 48
POOL = 4096
KVW = 2048
QKVW = 8192


def layout(key):
    group_total = R // REQ_DEV
    dealing = jax.random.permutation(jax.random.fold_in(key, 11), R).astype(jnp.int32)
    longest = POOL // 2
    rest = POOL - longest
    chosen = jax.random.randint(jax.random.fold_in(key, 13), (group_total, 1), 0, REQ_DEV, dtype=jnp.int32)
    slots = jnp.arange(REQ_DEV, dtype=jnp.int32)[None, :]
    is_long = (slots == chosen).astype(jnp.int32)
    is_filler = (slots == (chosen + 1) % REQ_DEV).astype(jnp.int32)
    weights = jax.random.randint(jax.random.fold_in(key, 12), (group_total, REQ_DEV), 1, 17, dtype=jnp.int32) * (1 - is_long)
    shares = weights * rest // jnp.sum(weights, axis=1, keepdims=True)
    shares = shares + is_filler * (rest - jnp.sum(shares, axis=1, keepdims=True)) + is_long * longest
    bounds = jnp.cumsum(shares, axis=1)
    tokens = jnp.arange(POOL, dtype=jnp.int32)
    owners = jnp.sum((tokens[None, None, :] >= bounds[:, :, None]).astype(jnp.int32), axis=1).astype(jnp.int32)
    lengths = jnp.zeros((R,), jnp.int32).at[dealing].set(shares.reshape(-1).astype(jnp.int32))
    return (dealing, lengths, owners)


def draw_dealing(key, part):
    return layout(key)[0]


def draw_lengths(key, part):
    return layout(key)[1]


def draw_token_owner(key, part):
    return layout(key)[2]


def draw_project_weight(key, part):
    head_order = jax.random.permutation(jax.random.fold_in(key, 21), H).astype(jnp.float32)
    head_scale = 3.0 * jnp.exp(head_order * (jnp.log(20.0) / (H - 1)))
    query_scale = jnp.repeat(head_scale, HD)
    column_scale = jnp.concatenate([query_scale, jnp.ones((2 * KVH * HD,), jnp.float32)])
    base_key = jax.random.fold_in(key, 22)
    base = jnp.clip(jax.random.normal(base_key, (D, QKVW), jnp.float32), -6.0, 6.0)
    return (base * D ** (-0.5) * column_scale[None, :]).astype(jnp.bfloat16)


def block_levels(key, dims, cuts, low, largest):
    loudness, own = 1.0, jax.random.fold_in(key, 6)
    for axis_at, blocks in cuts:
        steps = jnp.exp(jax.random.uniform(jax.random.fold_in(own, axis_at), (blocks,), jnp.float32, low / len(cuts), largest / len(cuts)))
        loudness = loudness * jnp.repeat(steps, dims[axis_at] // blocks).reshape([-1 if axis == axis_at else 1 for axis in range(len(dims))])
    return loudness


def normal_values(key, shape, width, most, shards=(), kind=jnp.bfloat16):
    entries = jax.random.normal(key, shape, jnp.float32) * width
    if len(shards) > 0:
        entries = block_levels(key, shape, shards, -0.22, 0.18) * entries
    return jnp.clip(entries, min=-most, max=most).astype(kind)


def setup_inputs(seed: int = 0) -> dict:
    arg_keys = jax.random.split(jax.random.key(seed), 16)
    return {
        "embedded": normal_values(arg_keys[0], (STEPS, R, D), 1.0, 6.0, ((1, 4),)),
        "cache_keys": normal_values(arg_keys[1], (R // REQ_DEV, POOL, KVW), 1.0, 6.0, ((0, 4), (1, 8))),
        "cache_values": normal_values(arg_keys[2], (R // REQ_DEV, POOL, KVW), 1.0, 6.0, ((0, 4), (1, 8))),
        "token_owner": draw_token_owner(jax.random.fold_in(arg_keys[15], 71), 0),
        "dealing": draw_dealing(jax.random.fold_in(arg_keys[15], 71), 0),
        "lengths": draw_lengths(jax.random.fold_in(arg_keys[15], 71), 0),
        "project_weight": draw_project_weight(jax.random.fold_in(arg_keys[15], 71), 0),
        "output_weight": normal_values(arg_keys[7], (H * HD, D), (H * HD) ** -0.5, 0.09375, ((0, 8),)),
        "gate_weight": normal_values(arg_keys[8], (D, FF), D ** -0.5, 0.09375, ((1, 32),)),
        "up_weight": normal_values(arg_keys[9], (D, FF), D ** -0.5, 0.09375, ((1, 32),)),
        "down_weight": normal_values(arg_keys[10], (FF, D), FF ** -0.5, 0.046875, ((0, 32),)),
        "gain_first": jnp.clip(1.0 + 0.18 * jax.random.normal(arg_keys[11], (D,), jnp.float32), 0.1, 1.9),
        "gain_second": jnp.clip(1.0 + 0.18 * jax.random.normal(arg_keys[12], (D,), jnp.float32), 0.1, 1.9),
        "gain_third": jnp.clip(1.0 + 0.18 * jax.random.normal(arg_keys[13], (D,), jnp.float32), 0.1, 1.9),
        "gain_fourth": jnp.clip(1.0 + 0.18 * jax.random.normal(arg_keys[14], (D,), jnp.float32), 0.1, 1.9),
    }


soft_cap = 50.0
epsilon = 1e-06

def rms_scale(values, gain):
    mean_square = lax.optimization_barrier(jnp.mean(values * values, axis=-1, keepdims=True))
    return values * lax.rsqrt(mean_square + epsilon) * gain

def rotate(values, positions):
    half_width = values.shape[-1] // 2
    freq_index = jnp.arange(half_width, dtype=jnp.float32)
    inverse = jnp.exp(freq_index * (-2.0 * math.log(10000.0) / values.shape[-1]))
    angles = positions[:, None] * inverse[None, :]
    cosine = jnp.cos(angles)[:, None, :]
    sine = jnp.sin(angles)[:, None, :]
    first_half = values[..., :half_width]
    second_half = values[..., half_width:]
    return jnp.concatenate([first_half * cosine - second_half * sine, second_half * cosine + first_half * sine], axis=-1)

def capped_weight(scores):
    return jnp.exp(soft_cap * jnp.tanh(scores / soft_cap))

def rounded(values):
    return lax.optimization_barrier(values.astype(jnp.bfloat16)).astype(jnp.float32)

def add_fresh(totals, outputs, queries, fresh_keys, fresh_values):
    for key_rows, value_rows in zip(fresh_keys, fresh_values):
        scores = lax.optimization_barrier(jnp.sum(queries.astype(jnp.float32) * key_rows.astype(jnp.float32)[:, :, None, :], axis=-1))
        weights = capped_weight(scores)
        totals = totals + weights
        outputs = outputs + rounded(weights)[..., None] * value_rows.astype(jnp.float32)[:, :, None, :]
    return (totals, outputs)

def cache_part(queries, key_pool, value_pool, owner_row):
    scores = jnp.einsum('igqd,tgd->igqt', queries.astype(jnp.float32), key_pool.astype(jnp.float32))
    owned_mask = owner_row[None, :] == jnp.arange(queries.shape[0], dtype=jnp.int32)[:, None]
    weights = jnp.where(owned_mask[:, None, None, :], capped_weight(scores), 0.0)
    totals = lax.optimization_barrier(jnp.sum(weights, axis=-1))
    outputs = jnp.einsum('igqt,tgd->igqd', rounded(weights), value_pool.astype(jnp.float32))
    return (totals, outputs)

def reference(embedded, cache_keys, cache_values, token_owner, dealing, lengths, project_weight, output_weight, gate_weight, up_weight, down_weight, gain_first, gain_second, gain_third, gain_fourth):
    groups = R // REQ_DEV
    group_size = H // KVH
    attention_width = H * HD
    base_positions = lengths[dealing]
    key_pools = cache_keys.reshape(groups, POOL, KVH, HD)
    value_pools = cache_values.reshape(groups, POOL, KVH, HD)
    fresh_keys = []
    fresh_values = []
    results = []
    for moment in range(STEPS):
        stream = embedded[moment].astype(jnp.float32)
        normed = rms_scale(stream, gain_first).astype(jnp.bfloat16)
        projected = jnp.dot(normed, project_weight, preferred_element_type=jnp.float32).astype(jnp.bfloat16)
        positions = (base_positions + moment).astype(jnp.float32)
        query_rows = projected[:, :attention_width].astype(jnp.float32).reshape(R, H, HD)
        queries = (rotate(query_rows, positions) * HD ** (-0.5)).astype(jnp.bfloat16)
        key_rows = projected[:, attention_width:attention_width + KVW].astype(jnp.float32).reshape(R, KVH, HD)
        fresh_keys.append(rotate(key_rows, positions).astype(jnp.bfloat16))
        fresh_values.append(projected[:, attention_width + KVW:].reshape(R, KVH, HD))
        grouped = queries.reshape(groups, REQ_DEV, KVH, group_size, HD)
        totals, outputs = lax.map(lambda operands: cache_part(*operands), (grouped, key_pools, value_pools, token_owner))
        totals = totals.reshape(R, KVH, group_size)
        outputs = outputs.reshape(R, KVH, group_size, HD)
        totals, outputs = add_fresh(totals, outputs, queries.reshape(R, KVH, group_size, HD), fresh_keys, fresh_values)
        attended = (outputs / totals[..., None]).reshape(R, attention_width).astype(jnp.bfloat16)
        mixed = jnp.dot(attended, output_weight, preferred_element_type=jnp.float32)
        middle = stream + rms_scale(mixed, gain_second)
        feed_input = rms_scale(middle, gain_third).astype(jnp.bfloat16)
        gate_part = jnp.dot(feed_input, gate_weight, preferred_element_type=jnp.float32)
        up_part = jnp.dot(feed_input, up_weight, preferred_element_type=jnp.float32)
        hidden = (jax.nn.gelu(gate_part, approximate=True) * up_part).astype(jnp.bfloat16)
        summed = jnp.dot(hidden, down_weight, preferred_element_type=jnp.float32)
        results.append((middle + rms_scale(summed, gain_fourth)).astype(jnp.bfloat16))
    return jnp.stack(results)
```

```python
import math

import jax
import jax.numpy as jnp
from jax import lax
from jax.experimental import pallas as pl
from jax.experimental.pallas import tpu as pltpu
from jax.sharding import PartitionSpec as P

H = 16
KVH = 8
HD = 256
STEPS = 4
MESH = pl.DeviceIdType.MESH


soft_cap = 50.0
epsilon = 1e-06


def rms_scale(values, gain):
    mean_square = jnp.mean(values * values, axis=-1, keepdims=True)
    return values * lax.rsqrt(mean_square + epsilon) * gain


def rotate(values, positions):
    half_width = values.shape[-1] // 2
    freq_index = jnp.arange(half_width, dtype=jnp.float32)
    inverse = jnp.exp(freq_index * (-2.0 * math.log(10000.0) / values.shape[-1]))
    angles = positions[:, None] * inverse[None, :]
    cosine = jnp.cos(angles)[:, None, :]
    sine = jnp.sin(angles)[:, None, :]
    first_half = values[..., :half_width]
    second_half = values[..., half_width:]
    return jnp.concatenate(
        [first_half * cosine - second_half * sine, second_half * cosine + first_half * sine],
        axis=-1,
    )


def capped_weight(scores):
    return jnp.exp(soft_cap * jnp.tanh(scores / soft_cap))


def rounded(values):
    return lax.optimization_barrier(values.astype(jnp.bfloat16)).astype(jnp.float32)


def body(
    embedded,
    cache_keys,
    cache_values,
    token_owner,
    dealing,
    lengths,
    project_weight,
    output_weight,
    gate_weight,
    up_weight,
    down_weight,
    gain_first,
    gain_second,
    gain_third,
    gain_fourth,
):
    row_count = embedded.shape[1]
    rows = STEPS * row_count
    width = embedded.shape[2]
    local_tokens = cache_keys.shape[1]
    value_width = cache_keys.shape[2]
    group_size = H // KVH
    attention_width = H * HD
    column_count = output_weight.shape[0]
    group_index = lax.axis_index("req")
    seq_index = lax.axis_index("seq")
    seq_size = lax.axis_size("seq")
    req_size = lax.axis_size("req")
    column_start = seq_index * column_count
    slot_requests = lax.dynamic_slice_in_dim(dealing, group_index * row_count, row_count)
    matches = slot_requests[:, None] == jnp.arange(dealing.shape[0], dtype=jnp.int32)[None, :]
    base_positions = jnp.sum(jnp.where(matches, lengths[None, :], 0), axis=1)
    positions = base_positions[None, :] + jnp.arange(STEPS, dtype=jnp.int32)[:, None]
    positions = positions.reshape(rows).astype(jnp.float32)
    key_pool = cache_keys[0].reshape(local_tokens, KVH, HD)
    value_pool = cache_values[0].reshape(local_tokens, KVH, HD)
    slots = jnp.tile(jnp.arange(row_count, dtype=jnp.int32), STEPS)
    moments = jnp.repeat(jnp.arange(STEPS, dtype=jnp.int32), row_count)
    owned_mask = token_owner[0][None, :] == slots[:, None]
    stream = embedded.reshape(rows, width).astype(jnp.float32)
    normed = rms_scale(stream, gain_first).astype(jnp.bfloat16)
    local_part = jnp.dot(normed, project_weight, preferred_element_type=jnp.float32).astype(
        jnp.bfloat16
    )
    projected = lax.all_gather(local_part, "seq", axis=1, tiled=True)
    query_rows = projected[:, :attention_width].astype(jnp.float32).reshape(rows, H, HD)
    queries = (rotate(query_rows, positions) * HD ** (-0.5)).astype(jnp.bfloat16)
    key_rows = (
        projected[:, attention_width : attention_width + value_width]
        .astype(jnp.float32)
        .reshape(rows, KVH, HD)
    )
    fresh_keys = rotate(key_rows, positions).astype(jnp.bfloat16)
    fresh_values = projected[:, attention_width + value_width :].reshape(rows, KVH, HD)
    grouped = queries.reshape(rows, KVH, group_size, HD)
    all_keys = jnp.concatenate([key_pool, fresh_keys], axis=0)
    all_values = jnp.concatenate([value_pool, fresh_values], axis=0)
    fresh_mask = (
        (slots[None, :] == slots[:, None])
        & (moments[None, :] <= moments[:, None])
        & (seq_index == 0)
    )
    mask = jnp.concatenate([owned_mask, fresh_mask], axis=1)
    scores = jnp.einsum("igqd,tgd->igqt", grouped, all_keys, preferred_element_type=jnp.float32)
    weights = jnp.where(mask[:, None, None, :], capped_weight(scores), 0.0)
    totals = lax.psum(jnp.sum(weights, axis=-1), "seq").reshape(rows, H)
    outputs = jnp.einsum(
        "igqt,tgd->igqd",
        weights.astype(jnp.bfloat16),
        all_values,
        preferred_element_type=jnp.float32,
    ).reshape(rows, attention_width)
    outputs = lax.psum_scatter(outputs, "seq", scatter_dimension=1, tiled=True)
    spread = jnp.repeat(totals, HD, axis=1)
    spread = lax.dynamic_slice_in_dim(spread, column_start, column_count, 1)
    attended = (outputs / spread).astype(jnp.bfloat16)
    partial = jnp.dot(attended, output_weight, preferred_element_type=jnp.float32)
    mixed = lax.psum(partial, "seq")
    middle = stream + rms_scale(mixed, gain_second)
    feed_input = rms_scale(middle, gain_third).astype(jnp.bfloat16)
    block_rows = lax.all_gather(feed_input, "req", axis=0, tiled=True)
    gate_part = jnp.dot(block_rows, gate_weight, preferred_element_type=jnp.float32)
    up_part = jnp.dot(block_rows, up_weight, preferred_element_type=jnp.float32)
    hidden = (jax.nn.gelu(gate_part, approximate=True) * up_part).astype(jnp.bfloat16)
    summed = jnp.dot(hidden, down_weight, preferred_element_type=jnp.float32)
    summed = lax.psum_scatter(summed, "req", scatter_dimension=0, tiled=True)
    summed = lax.psum(summed, "seq")
    results = (middle + rms_scale(summed, gain_fourth)).astype(jnp.bfloat16)
    return results.reshape(STEPS, row_count, width)


def group_kernel(
    owner_ref, cos_ref, sin_ref, g1_ref, g2_ref, g3_ref, g4_ref, emb_ref,
    wp_hbm, kc_hbm, vc_hbm, wo_hbm, wg_hbm, wu_hbm, wd_hbm,
    out_ref,
    wp, kc, vc, wo, wg, wu, wd,
    rows32, normed, qall, fresh, obuf, keep_b, recv_bx, send_bz, recv_bz, own_b,
    send_t, recv_t, mix32, send_cx, recv_cx, send_cz, recv_cz, own_c, mid,
    fbuf, xq, part, send_d0, recv_d0, send_d1, recv_d1, keep_d1, send_d2, recv_d2, keep_d2,
    send_d3, recv_d3, own_d, rbuf, res32,
    load_sem, send_sem, recv_sem,
):
    f32, bf16 = jnp.float32, jnp.bfloat16
    r, s = lax.axis_index("req"), lax.axis_index("seq")
    y, c = r // 2, r % 2
    z, x = s // 2, s % 2
    px, py, pc = (r, z * 2 + 1 - x), ((1 - y) * 2 + c, s), (y * 2 + 1 - c, s)

    def at_z(other):
        return (r, other * 2 + x)

    loads = []

    def load(src, dst):
        copy = pltpu.make_async_copy(src, dst, load_sem.at[len(loads)])
        copy.start()
        loads.append(copy)
        return copy

    load_p = [load(wp_hbm.at[:, HD * j : HD * (j + 1)], wp.at[j]) for j in range(4)]
    load_k = load(kc_hbm.at[0], kc)
    load_v = load(vc_hbm.at[0], vc)
    load_o = load(wo_hbm, wo)
    load_g = load(wg_hbm, wg)
    load_u = load(wu_hbm, wu)
    load_d = load(wd_hbm, wd)

    barrier = pltpu.get_barrier_semaphore()
    partners = [(r, (s + k) % 8) for k in range(1, 8)] + [py, pc]
    for partner in partners:
        pl.semaphore_signal(barrier, inc=1, device_id=partner, device_id_type=MESH)

    counts = {"send": 0, "recv": 0}
    pending = []

    def slots(n):
        base = counts["recv"]
        counts["recv"] += n
        return base

    def send(src, dst, rid, dev, cond=None):
        sid = counts["send"]
        counts["send"] += 1
        copy = pltpu.make_async_remote_copy(
            src_ref=src, dst_ref=dst, send_sem=send_sem.at[sid], recv_sem=recv_sem.at[rid],
            device_id=dev, device_id_type=MESH,
        )
        when(cond, copy.start)
        pending.append((cond, copy))

    def when(cond, fn):
        if cond is None:
            fn()
        else:
            pl.when(cond)(fn)

    def arrive(dst, rid, cond=None):
        copy = pltpu.make_async_remote_copy(
            src_ref=dst, dst_ref=dst, send_sem=send_sem.at[0], recv_sem=recv_sem.at[rid],
            device_id=px, device_id_type=MESH,
        )
        when(cond, copy.wait_recv)

    def pack(top, bottom):
        return jnp.concatenate([top, bottom], axis=0).astype(bf16)

    for step in range(STEPS):
        rows32[12 * step : 12 * step + 12, :] = emb_ref[step].astype(f32)
    for t in range(6):
        v = rows32[8 * t : 8 * t + 8, :]
        scale = lax.rsqrt(jnp.mean(v * v, axis=-1, keepdims=True) + epsilon)
        rows_v = v * scale * g1_ref[...]
        mix32[0, 8 * t : 8 * t + 8, :] = rows_v[:, :896]
        mix32[1, 8 * t : 8 * t + 8, :] = rows_v[:, 896:1792]
        mix32[2, 8 * t : 8 * t + 8, :] = rows_v[:, 1792:2688]
        mix32[3, 8 * t : 8 * t + 8, :] = rows_v[:, 2688:]
    for q in range(4):
        normed[:, 896 * q : 896 * q + 896] = mix32[q].astype(bf16)

    pl.semaphore_wait(barrier, len(partners))

    base = jnp.where(s < 4, 4 * s, 16)
    is_query = z < 2
    value_role = z == 3
    cosv = jnp.where(value_role, 1.0, cos_ref[...])
    sinv = jnp.where(value_role, 0.0, sin_ref[...])
    factor = jnp.where(is_query, HD ** (-0.5), 1.0)
    q_in, f_in = slots(16), slots(2)
    kv = jnp.maximum(z - 2, 0)
    for j in range(4):
        load_p[j].wait()
        proj = jnp.dot(normed[...], wp[j], preferred_element_type=f32).astype(bf16).astype(f32)
        a, b = proj[:, :128], proj[:, 128:]
        turned = jnp.concatenate([a * cosv - b * sinv, b * cosv + a * sinv], axis=1)
        qall[base + j] = (turned * factor).astype(bf16)
        head = qall.at[base + j]
        rid = q_in + jnp.minimum(base + j, 15)
        qdst = qall.at[jnp.minimum(base + j, 15)]
        send(head, qdst, rid, at_z(2), is_query)
        send(head, qdst, rid, at_z(1 - jnp.minimum(z, 1)), is_query)
        send(head, qdst, rid, px, is_query)
        e = 4 * x + j
        send(head, fresh.at[kv], f_in + kv, (r, e), (z >= 2) & (e != s))

        @pl.when((z >= 2) & (e == s))
        def _():
            fresh[kv] = qall[base + j]

    for j in range(4):
        for a in range(2):
            h = 8 * a + 4 * x + j
            arrive(qall.at[h], q_in + h, z != a)
            send(qall.at[h], qall.at[h], q_in + h, at_z(3), z == 2)
            send(qall.at[h], qall.at[h], q_in + h, px, z != a)

    row_slot = (lax.broadcasted_iota(jnp.int32, (96, 1), 0) % 48) % 12
    owned = owner_ref[...] == row_slot
    eye = lax.broadcasted_iota(jnp.int32, (96, 128), 0) == lax.broadcasted_iota(jnp.int32, (96, 128), 1)
    table_row = lax.broadcasted_iota(jnp.int32, (8, 128), 0)
    table = jnp.zeros((8, 128), f32)
    bx_in = slots(4)
    load_k.wait()
    load_v.wait()
    for column in range(2):
        cx = x if column == 0 else 1 - x
        if column == 1:
            for j in range(4):
                for a in range(2):
                    h = 8 * a + 4 * cx + j
                    arrive(qall.at[h], q_in + h)
        for away in range(2):
            jj = 1 - x if away == 0 else x
            for a in range(2):
                e = 4 * a + 2 * cx + jj
                zd = e // 2
                lanes = pl.ds(pl.multiple_of(e * HD, HD), HD)
                qe = qall[pl.ds(2 * e, 2)].reshape(96, HD)
                scores = lax.dot_general(qe, kc[:, lanes], (((1,), (1,)), ((), ())), preferred_element_type=f32)
                w = jnp.where(owned, capped_weight(scores), 0.0)
                total = jnp.sum(w, axis=-1, keepdims=True)
                line = jnp.sum(jnp.where(eye, total, 0.0), axis=0, keepdims=True)
                table = jnp.where(table_row == e, line, table)
                o = jnp.dot(w.astype(bf16), vc[:, lanes], preferred_element_type=f32)
                if away == 0:
                    obuf[zd] = o.astype(bf16)
                    send(obuf.at[zd], recv_bx.at[zd], bx_in + zd, px)
                else:
                    keep_b[zd] = o
    t_in = slots(8)
    send_t[...] = table
    for k in range(1, 8):
        send(send_t, recv_t.at[s], t_in + s, (r, (s + k) % 8))

    bz_in = slots(4)
    for first in (1 - x, x):
        for a in range(2):
            zd = 2 * a + first
            arrive(recv_bx.at[zd], bx_in + zd)
            v = keep_b[zd] + recv_bx[zd].astype(f32)

            @pl.when(zd == z)
            def _():
                own_b[...] = v

            @pl.when(zd != z)
            def _():
                send_bz[zd] = v.astype(bf16)

            send(send_bz.at[zd], recv_bz.at[z], bz_in + z, at_z(zd), zd != z)

    arrive(fresh.at[0], f_in, 4 + s // 4 != s)
    arrive(fresh.at[1], f_in + 1, 6 + s // 4 != s)
    qe = qall[pl.ds(2 * s, 2)].reshape(96, HD)
    scores = lax.dot_general(qe, fresh[0], (((1,), (1,)), ((), ())), preferred_element_type=f32)
    ri = lax.broadcasted_iota(jnp.int32, (96, 48), 0) % 48
    ci = lax.broadcasted_iota(jnp.int32, (96, 48), 1)
    seen = (ri % 12 == ci % 12) & (ci // 12 <= ri // 12)
    w = jnp.where(seen, capped_weight(scores), 0.0)
    totals = jnp.sum(w, axis=-1, keepdims=True)
    fresh_out = jnp.dot(w.astype(bf16), fresh[1], preferred_element_type=f32)

    for k in range(1, 8):
        src = (s + k) % 8
        arrive(recv_t.at[src], t_in + src)
        table = table + recv_t[src]
    line = jnp.sum(jnp.where(table_row == s, table, 0.0), axis=0, keepdims=True)
    totals = totals + jnp.sum(jnp.where(eye, line, 0.0), axis=-1, keepdims=True)
    outs = fresh_out + own_b[...]
    for k in range(1, 4):
        src = (z + k) % 4
        arrive(recv_bz.at[src], bz_in + src)
        outs = outs + recv_bz[src].astype(f32)
    attended = outs / totals
    attended = jnp.concatenate([attended[:48], attended[48:]], axis=1).astype(bf16)

    z0 = (x + c) % 2
    k_me = z - z0
    is_owner = (k_me >= 0) & (k_me <= 2)
    cx_in, cz_in = slots(2), slots(8)
    load_o.wait()
    for h in range(2):
        for q in (2 * h, 2 * h + 1):
            mix32[q] = jnp.dot(attended, wo[:, 896 * q : 896 * q + 896], preferred_element_type=f32)

        def tile(k, col):
            rows = pl.ds(pl.multiple_of(24 * col + 8 * k, 8), 8)
            return mix32[2 * h, rows, :], mix32[2 * h + 1, rows, :]

        for k in range(3):
            send_cx[h, k] = pack(*tile(k, 1 - x))
        send(send_cx.at[h], recv_cx.at[h], cx_in + h, px)
    for h in range(2):
        arrive(recv_cx.at[h], cx_in + h)
        for k in range(3):
            rows = pl.ds(pl.multiple_of(24 * x + 8 * k, 8), 8)
            v = jnp.concatenate([mix32[2 * h, rows, :], mix32[2 * h + 1, rows, :]], axis=0)
            v = v + recv_cx[h, k].astype(f32)

            @pl.when(z0 + k == z)
            def _():
                own_c[h] = v

            @pl.when(z0 + k != z)
            def _():
                send_cz[h, k] = v.astype(bf16)

            send(send_cz.at[h, k], recv_cz.at[h, z], cz_in + 4 * h + z, at_z(z0 + k), z0 + k != z)

    my_rows = pl.ds(pl.multiple_of(24 * x + 8 * jnp.clip(k_me, 0, 2), 8), 8)
    tr_own = r * 2 + x
    g_own = 3 * tr_own + jnp.clip(k_me, 0, 2)

    def quarters(buf, recv, rid):
        out = []
        for h in range(2):
            v = buf[h]
            for k in range(1, 4):
                src = (z + k) % 4
                arrive(recv.at[h, src], rid + 4 * h + src)
                v = v + recv[h, src].astype(f32)
            out += [v[:8], v[8:]]
        return out

    def mean_scale(parts):
        square = sum(jnp.sum(p * p, axis=-1, keepdims=True) for p in parts)
        return lax.rsqrt(square * (1.0 / 3584.0) + epsilon)

    def cols(q):
        return slice(896 * q, 896 * q + 896)

    @pl.when(is_owner)
    def _():
        mixed = quarters(own_c, recv_cz, cz_in)
        scale = mean_scale(mixed)
        middle = [rows32[my_rows, cols(q)] + mixed[q] * scale * g2_ref[:, cols(q)] for q in range(4)]
        scale = mean_scale(middle)
        for q in range(4):
            mid[q] = middle[q]
        feed = [middle[q] * scale * g3_ref[:, cols(q)] for q in range(4)]
        for h in range(2):
            fbuf[h, g_own] = pack(feed[2 * h], feed[2 * h + 1])

    fb_in, fc_in = slots(48), slots(8)

    def fsend(h, g, dev, cond=None):
        send(fbuf.at[h, g], fbuf.at[h, g], fb_in + 24 * h + g, dev, cond)

    def farrive(h, g, cond=None):
        arrive(fbuf.at[h, g], fb_in + 24 * h + g, cond)

    def fcore(h, yy, xx):
        tr = (yy * 2 + c) * 2 + xx
        blocks = fbuf.at[h, pl.ds(3 * tr, 3)]
        send(blocks, blocks, fc_in + 4 * h + 2 * yy + xx, pc)

    for h in range(2):
        for k in (2, 1, 3):
            fsend(h, g_own, at_z((z + k) % 4), is_owner)
    tr_x, tr_y = r * 2 + 1 - x, ((1 - y) * 2 + c) * 2 + x
    tr_xy = ((1 - y) * 2 + c) * 2 + 1 - x
    for k in range(3):
        for h in range(2):
            farrive(h, 3 * tr_own + k, z0 + k != z)
            for dev in (px, py) if h == 0 else (py, px):
                fsend(h, 3 * tr_own + k, dev)
    for h in range(2):
        fcore(h, y, x)
    for k in range(3):
        farrive(0, 3 * tr_x + k)
        fsend(0, 3 * tr_x + k, py)
        farrive(1, 3 * tr_y + k)
        fsend(1, 3 * tr_y + k, px)
    fcore(0, y, 1 - x)
    fcore(1, 1 - y, x)
    for k in range(3):
        farrive(0, 3 * tr_y + k)
    fcore(0, 1 - y, x)
    for k in range(3):
        farrive(1, 3 * tr_x + k)
    fcore(1, y, 1 - x)
    for h in range(2):
        for k in range(3):
            farrive(h, 3 * tr_xy + k)
        fcore(h, 1 - y, 1 - x)

    load_g.wait()
    load_u.wait()
    gate = up = None
    for h in range(2):
        for yy in range(2):
            for xx in range(2):
                tr = (yy * 2 + 1 - c) * 2 + xx
                arrive(fbuf.at[h, pl.ds(3 * tr, 3)], fc_in + 4 * h + 2 * yy + xx)
        for p in range(12):
            one, two = fbuf[h, 2 * p].astype(f32), fbuf[h, 2 * p + 1].astype(f32)
            xq[0, 16 * p : 16 * p + 16, :] = pack(one[:8], two[:8])
            xq[1, 16 * p : 16 * p + 16, :] = pack(one[8:], two[8:])
        for i in range(2):
            k_rows = slice(896 * (2 * h + i), 896 * (2 * h + i) + 896)
            gate_more = jnp.dot(xq[i], wg[k_rows, :], preferred_element_type=f32)
            up_more = jnp.dot(xq[i], wu[k_rows, :], preferred_element_type=f32)
            gate = gate_more if gate is None else gate + gate_more
            up = up_more if up is None else up + up_more
    bent = 0.5 * gate * (1.0 + jnp.tanh(math.sqrt(2.0 / math.pi) * (gate + 0.044715 * (gate * gate * gate))))
    hidden = (bent * up).astype(bf16)
    load_d.wait()
    d0_in, d1_in, d2_in, d3_in = slots(6), slots(6), slots(6), slots(8)

    def piece(h, core, yy, xx, k):
        rows = pl.ds(pl.multiple_of(8 * (((yy * 2 + core) * 2 + xx) * 3 + k), 8), 8)
        return part[2 * h, rows, :], part[2 * h + 1, rows, :]

    for h in range(2):
        for q in (2 * h, 2 * h + 1):
            part[q] = jnp.dot(hidden, wd[:, cols(q)], preferred_element_type=f32)
        for k in range(3):
            for yy in range(2):
                for xx in range(2):
                    send_d0[h, k, 2 * yy + xx] = pack(*piece(h, 1 - c, yy, xx, k))
            send(send_d0.at[h, k], recv_d0.at[h, k], d0_in + 3 * h + k, pc)

    def stage1(h, k):
        arrive(recv_d0.at[h, k], d0_in + 3 * h + k)
        for i in range(2):
            for side in range(2):
                yy, xx = ((1 - y if side == 0 else y), i) if h == 0 else (i, (1 - x if side == 0 else x))
                v = jnp.concatenate(piece(h, c, yy, xx, k), axis=0) + recv_d0[h, k, 2 * yy + xx].astype(f32)
                if side == 0:
                    send_d1[h, k, i] = v.astype(bf16)
                else:
                    keep_d1[h, k, i] = v
        send(send_d1.at[h, k], recv_d1.at[h, k], d1_in + 3 * h + k, py if h == 0 else px)

    def stage2(h, k):
        arrive(recv_d1.at[h, k], d1_in + 3 * h + k)
        mine = x if h == 0 else y
        v = keep_d1[h, k, 1 - mine] + recv_d1[h, k, 1 - mine].astype(f32)
        send_d2[h, k] = v.astype(bf16)
        keep_d2[h, k] = keep_d1[h, k, mine] + recv_d1[h, k, mine].astype(f32)
        send(send_d2.at[h, k], recv_d2.at[h, k], d2_in + 3 * h + k, px if h == 0 else py)

    def stage3(h, k):
        arrive(recv_d2.at[h, k], d2_in + 3 * h + k)
        v = keep_d2[h, k] + recv_d2[h, k].astype(f32)

        @pl.when(z0 + k == z)
        def _():
            own_d[h] = v

        @pl.when(z0 + k != z)
        def _():
            send_d3[h, k] = v.astype(bf16)

        send(send_d3.at[h, k], recv_d3.at[h, z], d3_in + 4 * h + z, at_z(z0 + k), z0 + k != z)

    for stage, k in ((stage1, 0), (stage1, 1), (stage2, 0), (stage1, 2), (stage2, 1), (stage3, 0), (stage2, 2), (stage3, 1), (stage3, 2)):
        for h in range(2):
            stage(h, k)

    t_own = 3 * x + jnp.clip(k_me, 0, 2)

    @pl.when(is_owner)
    def _():
        summed = quarters(own_d, recv_d3, d3_in)
        scale = mean_scale(summed)
        res = [mid[q] + summed[q] * scale * g4_ref[:, cols(q)] for q in range(4)]
        for h in range(2):
            rbuf[t_own, h] = pack(res[2 * h], res[2 * h + 1])

    rb_in = slots(6)

    def rsend(t, dev, cond=None):
        send(rbuf.at[t], rbuf.at[t], rb_in + t, dev, cond)

    for k in (2, 1, 3):
        rsend(t_own, at_z((z + k) % 4), is_owner)

    def place(t):
        rows = pl.ds(pl.multiple_of(8 * t, 8), 8)
        for h in range(2):
            v = rbuf[t, h].astype(f32)
            res32[rows, cols(2 * h)] = v[:8]
            res32[rows, cols(2 * h + 1)] = v[8:]

    for k in range(3):
        arrive(rbuf.at[3 * x + k], rb_in + 3 * x + k, z0 + k != z)
        rsend(3 * x + k, px)
    for k in range(3):
        place(3 * x + k)
    for k in range(3):
        t = 3 * (1 - x) + k
        arrive(rbuf.at[t], rb_in + t)
        place(t)
    for step in range(STEPS):
        out_ref[step] = res32[12 * step : 12 * step + 12, :].astype(bf16)

    for cond, copy in pending:
        when(cond, copy.wait_send)
    assert counts["send"] <= SENDS and counts["recv"] <= RECVS, counts


SENDS, RECVS, LOADS = 192, 192, 10


def grouped(
    embedded, cache_keys, cache_values, token_owner, dealing, lengths,
    project_weight, output_weight, gate_weight, up_weight, down_weight,
    gain_first, gain_second, gain_third, gain_fourth,
):
    f32, bf16 = jnp.float32, jnp.bfloat16
    row_count, width = embedded.shape[1], embedded.shape[2]
    group = lax.axis_index("req")
    requests = lax.dynamic_slice_in_dim(dealing, group * row_count, row_count)
    matches = requests[:, None] == jnp.arange(dealing.shape[0], dtype=jnp.int32)[None, :]
    base = jnp.sum(jnp.where(matches, lengths[None, :], 0), axis=1)
    positions = (base[None, :] + jnp.arange(STEPS, dtype=jnp.int32)[:, None]).reshape(-1).astype(f32)
    inverse = jnp.exp(jnp.arange(HD // 2, dtype=f32) * (-2.0 * math.log(10000.0) / HD))
    angles = positions[:, None] * inverse[None, :]
    vmem = pl.BlockSpec(memory_space=pltpu.VMEM)
    hbm = pl.BlockSpec(memory_space=pl.ANY)
    V = pltpu.VMEM
    scratch = [
        V((4, width, HD), bf16), V(cache_keys.shape[1:], bf16), V(cache_values.shape[1:], bf16),
        V(output_weight.shape, bf16), V(gate_weight.shape, bf16), V(up_weight.shape, bf16), V(down_weight.shape, bf16),
        V((48, width), f32), V((48, width), bf16), V((20, 48, HD), bf16), V((2, 48, HD), bf16),
        V((4, 96, HD), bf16), V((4, 96, HD), f32), V((4, 96, HD), bf16), V((4, 96, HD), bf16), V((4, 96, HD), bf16), V((96, HD), f32),
        V((8, 128), f32), V((8, 8, 128), f32), V((4, 48, 896), f32),
        V((2, 3, 16, 896), bf16), V((2, 3, 16, 896), bf16), V((2, 3, 16, 896), bf16), V((2, 4, 16, 896), bf16), V((2, 16, 896), f32), V((4, 8, 896), f32),
        V((2, 24, 16, 896), bf16), V((2, 192, 896), bf16), V((4, 192, 896), f32),
        V((2, 3, 4, 16, 896), bf16), V((2, 3, 4, 16, 896), bf16),
        V((2, 3, 2, 16, 896), bf16), V((2, 3, 2, 16, 896), bf16), V((2, 3, 2, 16, 896), f32),
        V((2, 3, 16, 896), bf16), V((2, 3, 16, 896), bf16), V((2, 3, 16, 896), f32),
        V((2, 3, 16, 896), bf16), V((2, 4, 16, 896), bf16), V((2, 16, 896), f32), V((6, 2, 16, 896), bf16), V((48, width), f32),
        pltpu.SemaphoreType.DMA((LOADS,)), pltpu.SemaphoreType.DMA((SENDS,)), pltpu.SemaphoreType.DMA((RECVS,)),
    ]
    return pl.pallas_call(
        group_kernel,
        out_shape=jax.ShapeDtypeStruct(embedded.shape, bf16),
        in_specs=[vmem] * 8 + [hbm] * 7,
        out_specs=vmem,
        scratch_shapes=scratch,
        name="decode_layer",
        compiler_params=pltpu.CompilerParams(collective_id=0, has_side_effects=True, vmem_limit_bytes=56 * 2**20),
    )(
        token_owner, jnp.cos(angles), jnp.sin(angles),
        gain_first[None, :], gain_second[None, :], gain_third[None, :], gain_fourth[None, :], embedded,
        project_weight, cache_keys, cache_values, output_weight, gate_weight, up_weight, down_weight,
    )


def solution(mesh):
    fits = mesh.shape["req"] == 4 and mesh.shape["seq"] == 8
    return jax.shard_map(
        grouped if fits else body,
        mesh=mesh,
        in_specs=(
            P(None, "req", None),
            P("req", "seq", None),
            P("req", "seq", None),
            P("req", "seq"),
            P(),
            P(),
            P(None, "seq"),
            P("seq", None),
            P(None, ("req", "seq")),
            P(None, ("req", "seq")),
            P(("req", "seq"), None),
            P(),
            P(),
            P(),
            P(),
        ),
        out_specs=P(None, "req", None),
        check_vma=False,
    )
```

```python
import math

import jax
import jax.numpy as jnp
from jax import lax
from jax.experimental import pallas as pl
from jax.experimental.pallas import tpu as pltpu
from jax.sharding import PartitionSpec as P

H = 16
KVH = 8
HD = 256
STEPS = 4
MESH = pl.DeviceIdType.MESH


soft_cap = 50.0
epsilon = 1e-06


def rms_scale(values, gain):
    mean_square = jnp.mean(values * values, axis=-1, keepdims=True)
    return values * lax.rsqrt(mean_square + epsilon) * gain


def rotate(values, positions):
    half_width = values.shape[-1] // 2
    freq_index = jnp.arange(half_width, dtype=jnp.float32)
    inverse = jnp.exp(freq_index * (-2.0 * math.log(10000.0) / values.shape[-1]))
    angles = positions[:, None] * inverse[None, :]
    cosine = jnp.cos(angles)[:, None, :]
    sine = jnp.sin(angles)[:, None, :]
    first_half = values[..., :half_width]
    second_half = values[..., half_width:]
    return jnp.concatenate(
        [first_half * cosine - second_half * sine, second_half * cosine + first_half * sine],
        axis=-1,
    )


def capped_weight(scores):
    return jnp.exp(soft_cap * jnp.tanh(scores / soft_cap))


def rounded(values):
    return lax.optimization_barrier(values.astype(jnp.bfloat16)).astype(jnp.float32)


def body(
    embedded,
    cache_keys,
    cache_values,
    token_owner,
    dealing,
    lengths,
    project_weight,
    output_weight,
    gate_weight,
    up_weight,
    down_weight,
    gain_first,
    gain_second,
    gain_third,
    gain_fourth,
):
    row_count = embedded.shape[1]
    rows = STEPS * row_count
    width = embedded.shape[2]
    local_tokens = cache_keys.shape[1]
    value_width = cache_keys.shape[2]
    group_size = H // KVH
    attention_width = H * HD
    column_count = output_weight.shape[0]
    group_index = lax.axis_index("req")
    seq_index = lax.axis_index("seq")
    seq_size = lax.axis_size("seq")
    req_size = lax.axis_size("req")
    column_start = seq_index * column_count
    slot_requests = lax.dynamic_slice_in_dim(dealing, group_index * row_count, row_count)
    matches = slot_requests[:, None] == jnp.arange(dealing.shape[0], dtype=jnp.int32)[None, :]
    base_positions = jnp.sum(jnp.where(matches, lengths[None, :], 0), axis=1)
    positions = base_positions[None, :] + jnp.arange(STEPS, dtype=jnp.int32)[:, None]
    positions = positions.reshape(rows).astype(jnp.float32)
    key_pool = cache_keys[0].reshape(local_tokens, KVH, HD)
    value_pool = cache_values[0].reshape(local_tokens, KVH, HD)
    slots = jnp.tile(jnp.arange(row_count, dtype=jnp.int32), STEPS)
    moments = jnp.repeat(jnp.arange(STEPS, dtype=jnp.int32), row_count)
    owned_mask = token_owner[0][None, :] == slots[:, None]
    stream = embedded.reshape(rows, width).astype(jnp.float32)
    normed = rms_scale(stream, gain_first).astype(jnp.bfloat16)
    local_part = jnp.dot(normed, project_weight, preferred_element_type=jnp.float32).astype(
        jnp.bfloat16
    )
    projected = lax.all_gather(local_part, "seq", axis=1, tiled=True)
    query_rows = projected[:, :attention_width].astype(jnp.float32).reshape(rows, H, HD)
    queries = (rotate(query_rows, positions) * HD ** (-0.5)).astype(jnp.bfloat16)
    key_rows = (
        projected[:, attention_width : attention_width + value_width]
        .astype(jnp.float32)
        .reshape(rows, KVH, HD)
    )
    fresh_keys = rotate(key_rows, positions).astype(jnp.bfloat16)
    fresh_values = projected[:, attention_width + value_width :].reshape(rows, KVH, HD)
    grouped = queries.reshape(rows, KVH, group_size, HD)
    all_keys = jnp.concatenate([key_pool, fresh_keys], axis=0)
    all_values = jnp.concatenate([value_pool, fresh_values], axis=0)
    fresh_mask = (
        (slots[None, :] == slots[:, None])
        & (moments[None, :] <= moments[:, None])
        & (seq_index == 0)
    )
    mask = jnp.concatenate([owned_mask, fresh_mask], axis=1)
    scores = jnp.einsum("igqd,tgd->igqt", grouped, all_keys, preferred_element_type=jnp.float32)
    weights = jnp.where(mask[:, None, None, :], capped_weight(scores), 0.0)
    totals = lax.psum(jnp.sum(weights, axis=-1), "seq").reshape(rows, H)
    outputs = jnp.einsum(
        "igqt,tgd->igqd",
        weights.astype(jnp.bfloat16),
        all_values,
        preferred_element_type=jnp.float32,
    ).reshape(rows, attention_width)
    outputs = lax.psum_scatter(outputs, "seq", scatter_dimension=1, tiled=True)
    spread = jnp.repeat(totals, HD, axis=1)
    spread = lax.dynamic_slice_in_dim(spread, column_start, column_count, 1)
    attended = (outputs / spread).astype(jnp.bfloat16)
    partial = jnp.dot(attended, output_weight, preferred_element_type=jnp.float32)
    mixed = lax.psum(partial, "seq")
    middle = stream + rms_scale(mixed, gain_second)
    feed_input = rms_scale(middle, gain_third).astype(jnp.bfloat16)
    block_rows = lax.all_gather(feed_input, "req", axis=0, tiled=True)
    gate_part = jnp.dot(block_rows, gate_weight, preferred_element_type=jnp.float32)
    up_part = jnp.dot(block_rows, up_weight, preferred_element_type=jnp.float32)
    hidden = (jax.nn.gelu(gate_part, approximate=True) * up_part).astype(jnp.bfloat16)
    summed = jnp.dot(hidden, down_weight, preferred_element_type=jnp.float32)
    summed = lax.psum_scatter(summed, "req", scatter_dimension=0, tiled=True)
    summed = lax.psum(summed, "seq")
    results = (middle + rms_scale(summed, gain_fourth)).astype(jnp.bfloat16)
    return results.reshape(STEPS, row_count, width)


def group_kernel(
    dealing_ref, lengths_ref, owner_ref, g1_ref, g2_ref, g3_ref, g4_ref, emb_ref,
    wp_hbm, kc_hbm, vc_hbm, wo_hbm, wg_hbm, wu_hbm, wd_hbm,
    out_ref,
    wp, kc, vc, wo, wg, wu, wd,
    rows32, normed, qall, fresh, obuf, keep_b, recv_bx, send_bz, recv_bz, own_b,
    send_t, recv_t, mix32, send_cx, recv_cx, send_cz, recv_cz, own_c, mid,
    fbuf, xq, part, send_d0, recv_d0, send_d1, recv_d1, keep_d1, send_d2, recv_d2, keep_d2,
    send_d3, recv_d3, own_d, rbuf,
    load_sem, send_sem, recv_sem,
):
    f32, bf16 = jnp.float32, jnp.bfloat16
    r, s = lax.axis_index("req"), lax.axis_index("seq")
    y, c = r // 2, r % 2
    z, x = s // 2, s % 2
    px, py, pc = (r, z * 2 + 1 - x), ((1 - y) * 2 + c, s), (y * 2 + 1 - c, s)

    def at_z(other):
        return (r, other * 2 + x)

    loads = []

    def load(src, dst):
        copy = pltpu.make_async_copy(src, dst, load_sem.at[len(loads)])
        copy.start()
        loads.append(copy)
        return copy

    load_p = [load(wp_hbm.at[:, HD * j : HD * (j + 1)], wp.at[j]) for j in range(4)]
    load_k = load(kc_hbm.at[0], kc)
    load_v = load(vc_hbm.at[0], vc)
    load_o = load(wo_hbm, wo)
    load_g = load(wg_hbm, wg)
    load_u = load(wu_hbm, wu)
    load_d = load(wd_hbm, wd)

    barrier = pltpu.get_barrier_semaphore()
    partners = [(r, (s + k) % 8) for k in range(1, 8)] + [py, pc]
    for partner in partners:
        pl.semaphore_signal(barrier, inc=1, device_id=partner, device_id_type=MESH)

    counts = {"send": 0, "recv": 0}
    pending = []

    def slots(n):
        base = counts["recv"]
        counts["recv"] += n
        return base

    def send(src, dst, rid, dev, cond=None):
        sid = counts["send"]
        counts["send"] += 1
        copy = pltpu.make_async_remote_copy(
            src_ref=src, dst_ref=dst, send_sem=send_sem.at[sid], recv_sem=recv_sem.at[rid],
            device_id=dev, device_id_type=MESH,
        )
        when(cond, copy.start)
        pending.append((cond, copy))

    def when(cond, fn):
        if cond is None:
            fn()
        else:
            pl.when(cond)(fn)

    def arrive(dst, rid, cond=None):
        copy = pltpu.make_async_remote_copy(
            src_ref=dst, dst_ref=dst, send_sem=send_sem.at[0], recv_sem=recv_sem.at[rid],
            device_id=px, device_id_type=MESH,
        )
        when(cond, copy.wait_recv)

    def pack(top, bottom):
        return jnp.concatenate([top, bottom], axis=0).astype(bf16)

    for t in range(6):
        rows32[8 * t : 8 * t + 8, :] = jnp.concatenate([emb_ref[2 * t].astype(f32), emb_ref[2 * t + 1].astype(f32)], axis=0)
    gain = g1_ref[...][None, :]
    for t in range(3):
        v = rows32[16 * t : 16 * t + 16, :]
        scale = lax.rsqrt(jnp.mean(v * v, axis=-1, keepdims=True) + epsilon)
        normed[16 * t : 16 * t + 16, :] = (v * scale * gain).astype(bf16)

    row = lax.broadcasted_iota(jnp.int32, (48, 128), 0)
    position = row % STEPS
    for i in range(12):
        position = position + jnp.where(row // STEPS == i, lengths_ref[dealing_ref[12 * r + i]], 0)
    lane = lax.broadcasted_iota(jnp.int32, (48, 128), 1).astype(f32)
    angles = position.astype(f32) * jnp.exp(lane * (-2.0 * math.log(10000.0) / HD))
    cosine, sine = jnp.cos(angles), jnp.sin(angles)

    pl.semaphore_wait(barrier, len(partners))

    base = jnp.where(s < 4, 4 * s, 16)
    is_query = z < 2
    value_role = z == 3
    cosv = jnp.where(value_role, 1.0, cosine)
    sinv = jnp.where(value_role, 0.0, sine)
    factor = jnp.where(is_query, HD ** (-0.5), 1.0)
    q_in, f_in = slots(16), slots(2)
    kv = jnp.maximum(z - 2, 0)
    for j in range(4):
        load_p[j].wait()
        proj = jnp.dot(normed[...], wp[j], preferred_element_type=f32).astype(bf16).astype(f32)
        a, b = proj[:, :128], proj[:, 128:]
        turned = jnp.concatenate([a * cosv - b * sinv, b * cosv + a * sinv], axis=1)
        qall[base + j] = (turned * factor).astype(bf16)
        head = qall.at[base + j]
        rid = q_in + jnp.minimum(base + j, 15)
        qdst = qall.at[jnp.minimum(base + j, 15)]
        send(head, qdst, rid, at_z(2), is_query)
        send(head, qdst, rid, at_z(1 - jnp.minimum(z, 1)), is_query)
        send(head, qdst, rid, px, is_query)
        e = 4 * x + j
        send(head, fresh.at[kv], f_in + kv, (r, e), (z >= 2) & (e != s))

        @pl.when((z >= 2) & (e == s))
        def _():
            fresh[kv] = qall[base + j]

    for j in range(4):
        for a in range(2):
            h = 8 * a + 4 * x + j
            arrive(qall.at[h], q_in + h, z != a)
            send(qall.at[h], qall.at[h], q_in + h, at_z(3), z == 2)
            send(qall.at[h], qall.at[h], q_in + h, px, z != a)

    row_slot = (lax.broadcasted_iota(jnp.int32, (96, 1), 0) % 48) // STEPS
    owned = owner_ref[...] == row_slot
    eye = lax.broadcasted_iota(jnp.int32, (96, 128), 0) == lax.broadcasted_iota(jnp.int32, (96, 128), 1)
    table_row = lax.broadcasted_iota(jnp.int32, (8, 128), 0)
    table = jnp.zeros((8, 128), f32)
    bx_in = slots(4)
    load_k.wait()
    load_v.wait()
    for column in range(2):
        cx = x if column == 0 else 1 - x
        if column == 1:
            for j in range(4):
                for a in range(2):
                    h = 8 * a + 4 * cx + j
                    arrive(qall.at[h], q_in + h)
        for away in range(2):
            jj = 1 - x if away == 0 else x
            for a in range(2):
                e = 4 * a + 2 * cx + jj
                zd = e // 2
                lanes = pl.ds(pl.multiple_of(e * HD, HD), HD)
                qe = qall[pl.ds(2 * e, 2)].reshape(96, HD)
                scores = lax.dot_general(qe, kc[:, lanes], (((1,), (1,)), ((), ())), preferred_element_type=f32)
                w = jnp.where(owned, capped_weight(scores), 0.0)
                total = jnp.sum(w, axis=-1, keepdims=True)
                line = jnp.sum(jnp.where(eye, total, 0.0), axis=0, keepdims=True)
                table = jnp.where(table_row == e, line, table)
                o = jnp.dot(w.astype(bf16), vc[:, lanes], preferred_element_type=f32)
                if away == 0:
                    obuf[zd] = o.astype(bf16)
                    send(obuf.at[zd], recv_bx.at[zd], bx_in + zd, px)
                else:
                    keep_b[zd] = o
    t_in = slots(8)
    send_t[...] = table
    for k in range(1, 8):
        send(send_t, recv_t.at[s], t_in + s, (r, (s + k) % 8))

    bz_in = slots(4)
    for first in (1 - x, x):
        for a in range(2):
            zd = 2 * a + first
            arrive(recv_bx.at[zd], bx_in + zd)
            v = keep_b[zd] + recv_bx[zd].astype(f32)

            @pl.when(zd == z)
            def _():
                own_b[...] = v

            @pl.when(zd != z)
            def _():
                send_bz[zd] = v.astype(bf16)

            send(send_bz.at[zd], recv_bz.at[z], bz_in + z, at_z(zd), zd != z)

    arrive(fresh.at[0], f_in, 4 + s // 4 != s)
    arrive(fresh.at[1], f_in + 1, 6 + s // 4 != s)
    qe = qall[pl.ds(2 * s, 2)].reshape(96, HD)
    scores = lax.dot_general(qe, fresh[0], (((1,), (1,)), ((), ())), preferred_element_type=f32)
    ri = lax.broadcasted_iota(jnp.int32, (96, 48), 0) % 48
    ci = lax.broadcasted_iota(jnp.int32, (96, 48), 1)
    seen = (ri // STEPS == ci // STEPS) & (ci % STEPS <= ri % STEPS)
    w = jnp.where(seen, capped_weight(scores), 0.0)
    totals = jnp.sum(w, axis=-1, keepdims=True)
    fresh_out = jnp.dot(w.astype(bf16), fresh[1], preferred_element_type=f32)

    for k in range(1, 8):
        src = (s + k) % 8
        arrive(recv_t.at[src], t_in + src)
        table = table + recv_t[src]
    line = jnp.sum(jnp.where(table_row == s, table, 0.0), axis=0, keepdims=True)
    totals = totals + jnp.sum(jnp.where(eye, line, 0.0), axis=-1, keepdims=True)
    outs = fresh_out + own_b[...]
    for k in range(1, 4):
        src = (z + k) % 4
        arrive(recv_bz.at[src], bz_in + src)
        outs = outs + recv_bz[src].astype(f32)
    attended = outs / totals
    attended = jnp.concatenate([attended[:48], attended[48:]], axis=1).astype(bf16)

    z0 = (x + c) % 2
    k_me = z - z0
    is_owner = (k_me >= 0) & (k_me <= 2)
    cx_in, cz_in = slots(2), slots(8)
    load_o.wait()
    for h in range(2):
        for q in (2 * h, 2 * h + 1):
            mix32[q] = jnp.dot(attended, wo[:, 896 * q : 896 * q + 896], preferred_element_type=f32)

        def tile(k, col):
            rows = pl.ds(pl.multiple_of(24 * col + 8 * k, 8), 8)
            return mix32[2 * h, rows, :], mix32[2 * h + 1, rows, :]

        for k in range(3):
            send_cx[h, k] = pack(*tile(k, 1 - x))
        send(send_cx.at[h], recv_cx.at[h], cx_in + h, px)
    for h in range(2):
        arrive(recv_cx.at[h], cx_in + h)
        for k in range(3):
            rows = pl.ds(pl.multiple_of(24 * x + 8 * k, 8), 8)
            v = jnp.concatenate([mix32[2 * h, rows, :], mix32[2 * h + 1, rows, :]], axis=0)
            v = v + recv_cx[h, k].astype(f32)

            @pl.when(z0 + k == z)
            def _():
                own_c[h] = v

            @pl.when(z0 + k != z)
            def _():
                send_cz[h, k] = v.astype(bf16)

            send(send_cz.at[h, k], recv_cz.at[h, z], cz_in + 4 * h + z, at_z(z0 + k), z0 + k != z)

    my_rows = pl.ds(pl.multiple_of(24 * x + 8 * jnp.clip(k_me, 0, 2), 8), 8)
    tr_own = r * 2 + x
    g_own = 3 * tr_own + jnp.clip(k_me, 0, 2)

    def quarters(buf, recv, rid):
        out = []
        for h in range(2):
            v = buf[h]
            for k in range(1, 4):
                src = (z + k) % 4
                arrive(recv.at[h, src], rid + 4 * h + src)
                v = v + recv[h, src].astype(f32)
            out += [v[:8], v[8:]]
        return out

    def mean_scale(parts):
        square = sum(jnp.sum(p * p, axis=-1, keepdims=True) for p in parts)
        return lax.rsqrt(square * (1.0 / 3584.0) + epsilon)

    def cols(q):
        return slice(896 * q, 896 * q + 896)

    @pl.when(is_owner)
    def _():
        mixed = quarters(own_c, recv_cz, cz_in)
        scale = mean_scale(mixed)
        middle = [rows32[my_rows, cols(q)] + mixed[q] * scale * g2_ref[cols(q)][None, :] for q in range(4)]
        scale = mean_scale(middle)
        for q in range(4):
            mid[q] = middle[q]
        feed = [middle[q] * scale * g3_ref[cols(q)][None, :] for q in range(4)]
        for h in range(2):
            fbuf[h, g_own] = pack(feed[2 * h], feed[2 * h + 1])

    fb_in, fc_in = slots(48), slots(8)

    def fsend(h, g, dev, cond=None):
        send(fbuf.at[h, g], fbuf.at[h, g], fb_in + 24 * h + g, dev, cond)

    def farrive(h, g, cond=None):
        arrive(fbuf.at[h, g], fb_in + 24 * h + g, cond)

    def fcore(h, yy, xx):
        tr = (yy * 2 + c) * 2 + xx
        blocks = fbuf.at[h, pl.ds(3 * tr, 3)]
        send(blocks, blocks, fc_in + 4 * h + 2 * yy + xx, pc)

    for h in range(2):
        for k in (2, 1, 3):
            fsend(h, g_own, at_z((z + k) % 4), is_owner)
    tr_x, tr_y = r * 2 + 1 - x, ((1 - y) * 2 + c) * 2 + x
    tr_xy = ((1 - y) * 2 + c) * 2 + 1 - x
    for k in range(3):
        for h in range(2):
            farrive(h, 3 * tr_own + k, z0 + k != z)
            for dev in (px, py) if h == 0 else (py, px):
                fsend(h, 3 * tr_own + k, dev)
    for h in range(2):
        fcore(h, y, x)
    for k in range(3):
        farrive(0, 3 * tr_x + k)
        fsend(0, 3 * tr_x + k, py)
        farrive(1, 3 * tr_y + k)
        fsend(1, 3 * tr_y + k, px)
    fcore(0, y, 1 - x)
    fcore(1, 1 - y, x)
    for k in range(3):
        farrive(0, 3 * tr_y + k)
    fcore(0, 1 - y, x)
    for k in range(3):
        farrive(1, 3 * tr_x + k)
    fcore(1, y, 1 - x)
    for h in range(2):
        for k in range(3):
            farrive(h, 3 * tr_xy + k)
        fcore(h, 1 - y, 1 - x)

    load_g.wait()
    load_u.wait()
    gate = up = None
    for h in range(2):
        for yy in range(2):
            for xx in range(2):
                tr = (yy * 2 + 1 - c) * 2 + xx
                arrive(fbuf.at[h, pl.ds(3 * tr, 3)], fc_in + 4 * h + 2 * yy + xx)
        for p in range(12):
            one, two = fbuf[h, 2 * p].astype(f32), fbuf[h, 2 * p + 1].astype(f32)
            xq[0, 16 * p : 16 * p + 16, :] = pack(one[:8], two[:8])
            xq[1, 16 * p : 16 * p + 16, :] = pack(one[8:], two[8:])
        for i in range(2):
            k_rows = slice(896 * (2 * h + i), 896 * (2 * h + i) + 896)
            gate_more = lax.dot_general(xq[i], wg[:, k_rows], (((1,), (1,)), ((), ())), preferred_element_type=f32)
            up_more = lax.dot_general(xq[i], wu[:, k_rows], (((1,), (1,)), ((), ())), preferred_element_type=f32)
            gate = gate_more if gate is None else gate + gate_more
            up = up_more if up is None else up + up_more
    bent = 0.5 * gate * (1.0 + jnp.tanh(math.sqrt(2.0 / math.pi) * (gate + 0.044715 * (gate * gate * gate))))
    hidden = (bent * up).astype(bf16)
    load_d.wait()
    d0_in, d1_in, d2_in, d3_in = slots(6), slots(6), slots(6), slots(8)

    def piece(h, core, yy, xx, k):
        rows = pl.ds(pl.multiple_of(8 * (((yy * 2 + core) * 2 + xx) * 3 + k), 8), 8)
        return part[2 * h, rows, :], part[2 * h + 1, rows, :]

    for h in range(2):
        for q in (2 * h, 2 * h + 1):
            part[q] = jnp.dot(hidden, wd[:, cols(q)], preferred_element_type=f32)
        for k in range(3):
            for yy in range(2):
                for xx in range(2):
                    send_d0[h, k, 2 * yy + xx] = pack(*piece(h, 1 - c, yy, xx, k))
            send(send_d0.at[h, k], recv_d0.at[h, k], d0_in + 3 * h + k, pc)

    def stage1(h, k):
        arrive(recv_d0.at[h, k], d0_in + 3 * h + k)
        for i in range(2):
            for side in range(2):
                yy, xx = ((1 - y if side == 0 else y), i) if h == 0 else (i, (1 - x if side == 0 else x))
                v = jnp.concatenate(piece(h, c, yy, xx, k), axis=0) + recv_d0[h, k, 2 * yy + xx].astype(f32)
                if side == 0:
                    send_d1[h, k, i] = v.astype(bf16)
                else:
                    keep_d1[h, k, i] = v
        send(send_d1.at[h, k], recv_d1.at[h, k], d1_in + 3 * h + k, py if h == 0 else px)

    def stage2(h, k):
        arrive(recv_d1.at[h, k], d1_in + 3 * h + k)
        mine = x if h == 0 else y
        v = keep_d1[h, k, 1 - mine] + recv_d1[h, k, 1 - mine].astype(f32)
        send_d2[h, k] = v.astype(bf16)
        keep_d2[h, k] = keep_d1[h, k, mine] + recv_d1[h, k, mine].astype(f32)
        send(send_d2.at[h, k], recv_d2.at[h, k], d2_in + 3 * h + k, px if h == 0 else py)

    def stage3(h, k):
        arrive(recv_d2.at[h, k], d2_in + 3 * h + k)
        v = keep_d2[h, k] + recv_d2[h, k].astype(f32)

        @pl.when(z0 + k == z)
        def _():
            own_d[h] = v

        @pl.when(z0 + k != z)
        def _():
            send_d3[h, k] = v.astype(bf16)

        send(send_d3.at[h, k], recv_d3.at[h, z], d3_in + 4 * h + z, at_z(z0 + k), z0 + k != z)

    for stage, k in ((stage1, 0), (stage1, 1), (stage2, 0), (stage1, 2), (stage2, 1), (stage3, 0), (stage2, 2), (stage3, 1), (stage3, 2)):
        for h in range(2):
            stage(h, k)

    t_own = 3 * x + jnp.clip(k_me, 0, 2)

    @pl.when(is_owner)
    def _():
        summed = quarters(own_d, recv_d3, d3_in)
        scale = mean_scale(summed)
        res = [mid[q] + summed[q] * scale * g4_ref[cols(q)][None, :] for q in range(4)]
        for h in range(2):
            rbuf[t_own, h] = pack(res[2 * h], res[2 * h + 1])

    rb_in = slots(6)

    def rsend(t, dev, cond=None):
        send(rbuf.at[t], rbuf.at[t], rb_in + t, dev, cond)

    for k in (2, 1, 3):
        rsend(t_own, at_z((z + k) % 4), is_owner)

    def place(t):
        for h in range(2):
            v = rbuf[t, h].astype(f32)
            for i in range(2):
                out_ref[2 * t, :, cols(2 * h + i)] = v[8 * i : 8 * i + 4].astype(bf16)
                out_ref[2 * t + 1, :, cols(2 * h + i)] = v[8 * i + 4 : 8 * i + 8].astype(bf16)

    for k in range(3):
        arrive(rbuf.at[3 * x + k], rb_in + 3 * x + k, z0 + k != z)
        rsend(3 * x + k, px)
    for k in range(3):
        place(3 * x + k)
    for k in range(3):
        t = 3 * (1 - x) + k
        arrive(rbuf.at[t], rb_in + t)
        place(t)
    for cond, copy in pending:
        when(cond, copy.wait_send)
    assert counts["send"] <= SENDS and counts["recv"] <= RECVS, counts


SENDS, RECVS, LOADS = 192, 192, 10


def grouped(
    embedded, cache_keys, cache_values, token_owner, dealing, lengths,
    project_weight, output_weight, gate_weight, up_weight, down_weight,
    gain_first, gain_second, gain_third, gain_fourth,
):
    f32, bf16 = jnp.float32, jnp.bfloat16
    width = embedded.shape[2]
    by_slot = embedded.transpose(1, 0, 2)
    gate_rows, up_rows = gate_weight.T, up_weight.T
    vmem = pl.BlockSpec(memory_space=pltpu.VMEM)
    hbm = pl.BlockSpec(memory_space=pl.ANY)
    V = pltpu.VMEM
    scratch = [
        V((4, width, HD), bf16), V(cache_keys.shape[1:], bf16), V(cache_values.shape[1:], bf16),
        V(output_weight.shape, bf16), V(gate_rows.shape, bf16), V(up_rows.shape, bf16), V(down_weight.shape, bf16),
        V((48, width), f32), V((48, width), bf16), V((20, 48, HD), bf16), V((2, 48, HD), bf16),
        V((4, 96, HD), bf16), V((4, 96, HD), f32), V((4, 96, HD), bf16), V((4, 96, HD), bf16), V((4, 96, HD), bf16), V((96, HD), f32),
        V((8, 128), f32), V((8, 8, 128), f32), V((4, 48, 896), f32),
        V((2, 3, 16, 896), bf16), V((2, 3, 16, 896), bf16), V((2, 3, 16, 896), bf16), V((2, 4, 16, 896), bf16), V((2, 16, 896), f32), V((4, 8, 896), f32),
        V((2, 24, 16, 896), bf16), V((2, 192, 896), bf16), V((4, 192, 896), f32),
        V((2, 3, 4, 16, 896), bf16), V((2, 3, 4, 16, 896), bf16),
        V((2, 3, 2, 16, 896), bf16), V((2, 3, 2, 16, 896), bf16), V((2, 3, 2, 16, 896), f32),
        V((2, 3, 16, 896), bf16), V((2, 3, 16, 896), bf16), V((2, 3, 16, 896), f32),
        V((2, 3, 16, 896), bf16), V((2, 4, 16, 896), bf16), V((2, 16, 896), f32), V((6, 2, 16, 896), bf16),
        pltpu.SemaphoreType.DMA((LOADS,)), pltpu.SemaphoreType.DMA((SENDS,)), pltpu.SemaphoreType.DMA((RECVS,)),
    ]
    smem = pl.BlockSpec(memory_space=pltpu.SMEM)
    results = pl.pallas_call(
        group_kernel,
        out_shape=jax.ShapeDtypeStruct(by_slot.shape, bf16),
        in_specs=[smem] * 2 + [vmem] * 6 + [hbm] * 7,
        out_specs=vmem,
        scratch_shapes=scratch,
        name="decode_layer",
        compiler_params=pltpu.CompilerParams(collective_id=0, has_side_effects=True, vmem_limit_bytes=56 * 2**20),
    )(
        dealing, lengths, token_owner, gain_first, gain_second, gain_third, gain_fourth, by_slot,
        project_weight, cache_keys, cache_values, output_weight, gate_rows, up_rows, down_weight,
    )
    return results.transpose(1, 0, 2)


def solution(mesh):
    fits = mesh.shape["req"] == 4 and mesh.shape["seq"] == 8
    return jax.shard_map(
        grouped if fits else body,
        mesh=mesh,
        in_specs=(
            P(None, "req", None),
            P("req", "seq", None),
            P("req", "seq", None),
            P("req", "seq"),
            P(),
            P(),
            P(None, "seq"),
            P("seq", None),
            P(None, ("req", "seq")),
            P(None, ("req", "seq")),
            P(("req", "seq"), None),
            P(),
            P(),
            P(),
            P(),
        ),
        out_specs=P(None, "req", None),
        check_vma=False,
    )
```

```python
import math

import jax
import jax.numpy as jnp
from jax import lax
from jax.experimental import pallas as pl
from jax.experimental.pallas import tpu as pltpu
from jax.sharding import PartitionSpec as P

H = 16
KVH = 8
HD = 256
STEPS = 4
MESH = pl.DeviceIdType.MESH


soft_cap = 50.0
epsilon = 1e-06


def rms_scale(values, gain):
    mean_square = jnp.mean(values * values, axis=-1, keepdims=True)
    return values * lax.rsqrt(mean_square + epsilon) * gain


def rotate(values, positions):
    half_width = values.shape[-1] // 2
    freq_index = jnp.arange(half_width, dtype=jnp.float32)
    inverse = jnp.exp(freq_index * (-2.0 * math.log(10000.0) / values.shape[-1]))
    angles = positions[:, None] * inverse[None, :]
    cosine = jnp.cos(angles)[:, None, :]
    sine = jnp.sin(angles)[:, None, :]
    first_half = values[..., :half_width]
    second_half = values[..., half_width:]
    return jnp.concatenate(
        [first_half * cosine - second_half * sine, second_half * cosine + first_half * sine],
        axis=-1,
    )


def capped_weight(scores):
    return jnp.exp(soft_cap * jnp.tanh(scores / soft_cap))


def rounded(values):
    return lax.optimization_barrier(values.astype(jnp.bfloat16)).astype(jnp.float32)


def body(
    embedded,
    cache_keys,
    cache_values,
    token_owner,
    dealing,
    lengths,
    project_weight,
    output_weight,
    gate_weight,
    up_weight,
    down_weight,
    gain_first,
    gain_second,
    gain_third,
    gain_fourth,
):
    row_count = embedded.shape[1]
    rows = STEPS * row_count
    width = embedded.shape[2]
    local_tokens = cache_keys.shape[1]
    value_width = cache_keys.shape[2]
    group_size = H // KVH
    attention_width = H * HD
    column_count = output_weight.shape[0]
    group_index = lax.axis_index("req")
    seq_index = lax.axis_index("seq")
    seq_size = lax.axis_size("seq")
    req_size = lax.axis_size("req")
    column_start = seq_index * column_count
    slot_requests = lax.dynamic_slice_in_dim(dealing, group_index * row_count, row_count)
    matches = slot_requests[:, None] == jnp.arange(dealing.shape[0], dtype=jnp.int32)[None, :]
    base_positions = jnp.sum(jnp.where(matches, lengths[None, :], 0), axis=1)
    positions = base_positions[None, :] + jnp.arange(STEPS, dtype=jnp.int32)[:, None]
    positions = positions.reshape(rows).astype(jnp.float32)
    key_pool = cache_keys[0].reshape(local_tokens, KVH, HD)
    value_pool = cache_values[0].reshape(local_tokens, KVH, HD)
    slots = jnp.tile(jnp.arange(row_count, dtype=jnp.int32), STEPS)
    moments = jnp.repeat(jnp.arange(STEPS, dtype=jnp.int32), row_count)
    owned_mask = token_owner[0][None, :] == slots[:, None]
    stream = embedded.reshape(rows, width).astype(jnp.float32)
    normed = rms_scale(stream, gain_first).astype(jnp.bfloat16)
    local_part = jnp.dot(normed, project_weight, preferred_element_type=jnp.float32).astype(
        jnp.bfloat16
    )
    projected = lax.all_gather(local_part, "seq", axis=1, tiled=True)
    query_rows = projected[:, :attention_width].astype(jnp.float32).reshape(rows, H, HD)
    queries = (rotate(query_rows, positions) * HD ** (-0.5)).astype(jnp.bfloat16)
    key_rows = (
        projected[:, attention_width : attention_width + value_width]
        .astype(jnp.float32)
        .reshape(rows, KVH, HD)
    )
    fresh_keys = rotate(key_rows, positions).astype(jnp.bfloat16)
    fresh_values = projected[:, attention_width + value_width :].reshape(rows, KVH, HD)
    grouped = queries.reshape(rows, KVH, group_size, HD)
    all_keys = jnp.concatenate([key_pool, fresh_keys], axis=0)
    all_values = jnp.concatenate([value_pool, fresh_values], axis=0)
    fresh_mask = (
        (slots[None, :] == slots[:, None])
        & (moments[None, :] <= moments[:, None])
        & (seq_index == 0)
    )
    mask = jnp.concatenate([owned_mask, fresh_mask], axis=1)
    scores = jnp.einsum("igqd,tgd->igqt", grouped, all_keys, preferred_element_type=jnp.float32)
    weights = jnp.where(mask[:, None, None, :], capped_weight(scores), 0.0)
    totals = lax.psum(jnp.sum(weights, axis=-1), "seq").reshape(rows, H)
    outputs = jnp.einsum(
        "igqt,tgd->igqd",
        weights.astype(jnp.bfloat16),
        all_values,
        preferred_element_type=jnp.float32,
    ).reshape(rows, attention_width)
    outputs = lax.psum_scatter(outputs, "seq", scatter_dimension=1, tiled=True)
    spread = jnp.repeat(totals, HD, axis=1)
    spread = lax.dynamic_slice_in_dim(spread, column_start, column_count, 1)
    attended = (outputs / spread).astype(jnp.bfloat16)
    partial = jnp.dot(attended, output_weight, preferred_element_type=jnp.float32)
    mixed = lax.psum(partial, "seq")
    middle = stream + rms_scale(mixed, gain_second)
    feed_input = rms_scale(middle, gain_third).astype(jnp.bfloat16)
    block_rows = lax.all_gather(feed_input, "req", axis=0, tiled=True)
    gate_part = jnp.dot(block_rows, gate_weight, preferred_element_type=jnp.float32)
    up_part = jnp.dot(block_rows, up_weight, preferred_element_type=jnp.float32)
    hidden = (jax.nn.gelu(gate_part, approximate=True) * up_part).astype(jnp.bfloat16)
    summed = jnp.dot(hidden, down_weight, preferred_element_type=jnp.float32)
    summed = lax.psum_scatter(summed, "req", scatter_dimension=0, tiled=True)
    summed = lax.psum(summed, "seq")
    results = (middle + rms_scale(summed, gain_fourth)).astype(jnp.bfloat16)
    return results.reshape(STEPS, row_count, width)


def group_kernel(
    dealing_hbm, lengths_hbm, owner_hbm, g1_hbm, g2_hbm, g3_hbm, g4_hbm, emb_hbm,
    wp_hbm, kc_hbm, vc_hbm, wo_hbm, wg_hbm, wu_hbm, wd_hbm,
    out_ref,
    dealing_ref, lengths_ref, owner_ref, g1_ref, g2_ref, g3_ref, g4_ref, emb_ref,
    wp, kc, vc, wo, wg, wu, wd,
    rows32, normed, qall, fresh, obuf, keep_b, recv_bx, send_bz, recv_bz, own_b,
    send_t, recv_t, mix32, send_cx, recv_cx, send_cz, recv_cz, own_c, mid,
    fbuf, xq, part, send_d0, recv_d0, send_d1, recv_d1, keep_d1, send_d3, recv_d3, own_d, rbuf,
    load_sem, send_sem, recv_sem,
):
    f32, bf16 = jnp.float32, jnp.bfloat16
    r, s = lax.axis_index("req"), lax.axis_index("seq")
    y, c = r // 2, r % 2
    z, x = s // 2, s % 2
    px, py, pc = (r, z * 2 + 1 - x), ((1 - y) * 2 + c, s), (y * 2 + 1 - c, s)

    def at_z(other):
        return (r, other * 2 + x)

    barrier = pltpu.get_barrier_semaphore()
    partners = [(r, (s + k) % 8) for k in range(1, 8)] + [py, pc]
    for partner in partners:
        pl.semaphore_signal(barrier, inc=1, device_id=partner, device_id_type=MESH)

    loads = []

    def load(src, dst):
        copy = pltpu.make_async_copy(src, dst, load_sem.at[len(loads)])
        copy.start()
        loads.append(copy)
        return copy

    small = [
        load(emb_hbm, emb_ref), load(g1_hbm, g1_ref), load(dealing_hbm, dealing_ref), load(lengths_hbm, lengths_ref),
        load(owner_hbm, owner_ref), load(g2_hbm, g2_ref), load(g3_hbm, g3_ref), load(g4_hbm, g4_ref),
    ]
    load_p = [load(wp_hbm.at[:, HD * j : HD * (j + 1)], wp.at[j]) for j in range(4)]
    load_k = load(kc_hbm.at[0], kc)
    load_v = load(vc_hbm.at[0], vc)
    load_o = load(wo_hbm, wo)
    load_g = load(wg_hbm, wg)
    load_u = load(wu_hbm, wu)
    load_d = load(wd_hbm, wd)

    counts = {"send": 0, "recv": 0}
    pending = []

    def slots(n):
        base = counts["recv"]
        counts["recv"] += n
        return base

    def send(src, dst, rid, dev, cond=None):
        sid = counts["send"]
        counts["send"] += 1
        copy = pltpu.make_async_remote_copy(
            src_ref=src, dst_ref=dst, send_sem=send_sem.at[sid], recv_sem=recv_sem.at[rid],
            device_id=dev, device_id_type=MESH,
        )
        when(cond, copy.start)
        pending.append((cond, copy))

    def when(cond, fn):
        if cond is None:
            fn()
        else:
            pl.when(cond)(fn)

    def arrive(dst, rid, cond=None):
        copy = pltpu.make_async_remote_copy(
            src_ref=dst, dst_ref=dst, send_sem=send_sem.at[0], recv_sem=recv_sem.at[rid],
            device_id=px, device_id_type=MESH,
        )
        when(cond, copy.wait_recv)

    def pack(top, bottom):
        return jnp.concatenate([top, bottom], axis=0).astype(bf16)

    for copy in small:
        copy.wait()
    for t in range(6):
        rows32[8 * t : 8 * t + 8, :] = jnp.concatenate([emb_ref[2 * t].astype(f32), emb_ref[2 * t + 1].astype(f32)], axis=0)
    gain = g1_ref[...][None, :]
    for t in range(3):
        v = rows32[16 * t : 16 * t + 16, :]
        scale = lax.rsqrt(jnp.mean(v * v, axis=-1, keepdims=True) + epsilon)
        normed[16 * t : 16 * t + 16, :] = (v * scale * gain).astype(bf16)

    row = lax.broadcasted_iota(jnp.int32, (48, 128), 0)
    position = row % STEPS
    for i in range(12):
        position = position + jnp.where(row // STEPS == i, lengths_ref[dealing_ref[12 * r + i]], 0)
    lane = lax.broadcasted_iota(jnp.int32, (48, 128), 1).astype(f32)
    angles = position.astype(f32) * jnp.exp(lane * (-2.0 * math.log(10000.0) / HD))
    cosine, sine = jnp.cos(angles), jnp.sin(angles)

    base = jnp.where(s < 4, 4 * s, 16)
    is_query = z < 2
    value_role = z == 3
    cosv = jnp.where(value_role, 1.0, cosine)
    sinv = jnp.where(value_role, 0.0, sine)
    factor = jnp.where(is_query, HD ** (-0.5), 1.0)
    q_in, f_in = slots(16), slots(2)
    kv = jnp.maximum(z - 2, 0)
    for j in range(4):
        load_p[j].wait()
        proj = jnp.dot(normed[...], wp[j], preferred_element_type=f32).astype(bf16).astype(f32)
        a, b = proj[:, :128], proj[:, 128:]
        turned = jnp.concatenate([a * cosv - b * sinv, b * cosv + a * sinv], axis=1)
        qall[base + j] = (turned * factor).astype(bf16)
    pl.semaphore_wait(barrier, len(partners))
    for j in range(4):
        head = qall.at[base + j]
        rid = q_in + jnp.minimum(base + j, 15)
        qdst = qall.at[jnp.minimum(base + j, 15)]
        send(head, qdst, rid, at_z(2), is_query)
        send(head, qdst, rid, at_z(1 - jnp.minimum(z, 1)), is_query)
        send(head, qdst, rid, px, is_query)
        e = 4 * x + j
        send(head, fresh.at[kv], f_in + kv, (r, e), (z >= 2) & (e != s))

        @pl.when((z >= 2) & (e == s))
        def _():
            fresh[kv] = qall[base + j]

    for j in range(4):
        for a in range(2):
            h = 8 * a + 4 * x + j
            arrive(qall.at[h], q_in + h, z != a)
            send(qall.at[h], qall.at[h], q_in + h, at_z(3), z == 2)
            send(qall.at[h], qall.at[h], q_in + h, px, z != a)

    row_slot = (lax.broadcasted_iota(jnp.int32, (96, 1), 0) % 48) // STEPS
    owned = owner_ref[...] == row_slot
    eye = lax.broadcasted_iota(jnp.int32, (96, 128), 0) == lax.broadcasted_iota(jnp.int32, (96, 128), 1)
    table_row = lax.broadcasted_iota(jnp.int32, (8, 128), 0)
    table = jnp.zeros((8, 128), f32)
    bx_in = slots(4)
    load_k.wait()
    load_v.wait()
    for column in range(2):
        cx = x if column == 0 else 1 - x
        if column == 1:
            for j in range(4):
                for a in range(2):
                    h = 8 * a + 4 * cx + j
                    arrive(qall.at[h], q_in + h)
        for away in range(2):
            jj = 1 - x if away == 0 else x
            for a in range(2):
                e = 4 * a + 2 * cx + jj
                zd = e // 2
                lanes = pl.ds(pl.multiple_of(e * HD, HD), HD)
                qe = qall[pl.ds(2 * e, 2)].reshape(96, HD)
                scores = lax.dot_general(qe, kc[:, lanes], (((1,), (1,)), ((), ())), preferred_element_type=f32)
                w = jnp.where(owned, capped_weight(scores), 0.0)
                total = jnp.sum(w, axis=-1, keepdims=True)
                line = jnp.sum(jnp.where(eye, total, 0.0), axis=0, keepdims=True)
                table = jnp.where(table_row == e, line, table)
                o = jnp.dot(w.astype(bf16), vc[:, lanes], preferred_element_type=f32)
                if away == 0:
                    obuf[zd] = o.astype(bf16)
                    send(obuf.at[zd], recv_bx.at[zd], bx_in + zd, px)
                else:
                    keep_b[zd] = o
    t_in = slots(8)
    send_t[...] = table
    for k in range(1, 8):
        send(send_t, recv_t.at[s], t_in + s, (r, (s + k) % 8))

    bz_in = slots(4)
    for first in (1 - x, x):
        for a in range(2):
            zd = 2 * a + first
            arrive(recv_bx.at[zd], bx_in + zd)
            v = keep_b[zd] + recv_bx[zd].astype(f32)

            @pl.when(zd == z)
            def _():
                own_b[...] = v

            @pl.when(zd != z)
            def _():
                send_bz[zd] = v.astype(bf16)

            send(send_bz.at[zd], recv_bz.at[z], bz_in + z, at_z(zd), zd != z)

    arrive(fresh.at[0], f_in, 4 + s // 4 != s)
    arrive(fresh.at[1], f_in + 1, 6 + s // 4 != s)
    qe = qall[pl.ds(2 * s, 2)].reshape(96, HD)
    scores = lax.dot_general(qe, fresh[0], (((1,), (1,)), ((), ())), preferred_element_type=f32)
    ri = lax.broadcasted_iota(jnp.int32, (96, 48), 0) % 48
    ci = lax.broadcasted_iota(jnp.int32, (96, 48), 1)
    seen = (ri // STEPS == ci // STEPS) & (ci % STEPS <= ri % STEPS)
    w = jnp.where(seen, capped_weight(scores), 0.0)
    totals = jnp.sum(w, axis=-1, keepdims=True)
    fresh_out = jnp.dot(w.astype(bf16), fresh[1], preferred_element_type=f32)

    for k in range(1, 8):
        src = (s + k) % 8
        arrive(recv_t.at[src], t_in + src)
        table = table + recv_t[src]
    line = jnp.sum(jnp.where(table_row == s, table, 0.0), axis=0, keepdims=True)
    totals = totals + jnp.sum(jnp.where(eye, line, 0.0), axis=-1, keepdims=True)
    outs = fresh_out + own_b[...]
    for k in range(1, 4):
        src = (z + k) % 4
        arrive(recv_bz.at[src], bz_in + src)
        outs = outs + recv_bz[src].astype(f32)
    attended = outs / totals
    attended = jnp.concatenate([attended[:48], attended[48:]], axis=1).astype(bf16)

    z0 = (x + c) % 2
    k_me = z - z0
    is_owner = (k_me >= 0) & (k_me <= 2)
    cx_in, cz_in = slots(2), slots(8)
    load_o.wait()
    for h in range(2):
        for q in (2 * h, 2 * h + 1):
            mix32[q] = jnp.dot(attended, wo[:, 896 * q : 896 * q + 896], preferred_element_type=f32)

        def tile(k, col):
            rows = pl.ds(pl.multiple_of(24 * col + 8 * k, 8), 8)
            return mix32[2 * h, rows, :], mix32[2 * h + 1, rows, :]

        for k in range(3):
            send_cx[h, k] = pack(*tile(k, 1 - x))
        send(send_cx.at[h], recv_cx.at[h], cx_in + h, px)
    for h in range(2):
        arrive(recv_cx.at[h], cx_in + h)
        for k in range(3):
            rows = pl.ds(pl.multiple_of(24 * x + 8 * k, 8), 8)
            v = jnp.concatenate([mix32[2 * h, rows, :], mix32[2 * h + 1, rows, :]], axis=0)
            v = v + recv_cx[h, k].astype(f32)

            @pl.when(z0 + k == z)
            def _():
                own_c[h] = v

            @pl.when(z0 + k != z)
            def _():
                send_cz[h, k] = v.astype(bf16)

            send(send_cz.at[h, k], recv_cz.at[h, z], cz_in + 4 * h + z, at_z(z0 + k), z0 + k != z)

    my_rows = pl.ds(pl.multiple_of(24 * x + 8 * jnp.clip(k_me, 0, 2), 8), 8)
    k_own = jnp.clip(k_me, 0, 2)
    here = 2 * y + x

    def quarters(buf, recv, rid):
        out = []
        for h in range(2):
            v = buf[h]
            for k in range(1, 4):
                src = (z + k) % 4
                arrive(recv.at[h, src], rid + 4 * h + src)
                v = v + recv[h, src].astype(f32)
            out += [v[:8], v[8:]]
        return out

    def mean_scale(parts):
        square = sum(jnp.sum(p * p, axis=-1, keepdims=True) for p in parts)
        return lax.rsqrt(square * (1.0 / 3584.0) + epsilon)

    def cols(q):
        return slice(896 * q, 896 * q + 896)

    @pl.when(is_owner)
    def _():
        mixed = quarters(own_c, recv_cz, cz_in)
        scale = mean_scale(mixed)
        middle = [rows32[my_rows, cols(q)] + mixed[q] * scale * g2_ref[cols(q)][None, :] for q in range(4)]
        scale = mean_scale(middle)
        for q in range(4):
            mid[q] = middle[q]
        feed = [middle[q] * scale * g3_ref[cols(q)][None, :] for q in range(4)]
        for h in range(2):
            fbuf[k_own, c, here, h] = pack(feed[2 * h], feed[2 * h + 1])

    fb_in, fc_in = slots(12), slots(3)
    d0_in, d1_in, d3_in, rb_in = slots(6), slots(12), slots(4), slots(6)
    corner = ((1 - y) * 2 + c, z * 2 + 1 - x)
    beside_at, across_at, corner_at = 2 * y + 1 - x, 2 * (1 - y) + x, 2 * (1 - y) + 1 - x

    def fsend(k, dev, cond=None):
        block = fbuf.at[k, c, here]
        send(block, block, fb_in + 4 * k + here, dev, cond)

    def farrive(k, place, cond=None):
        arrive(fbuf.at[k, c, place], fb_in + 4 * k + place, cond)

    for far in (2, 1, 3):
        fsend(k_own, at_z((z + far) % 4), is_owner)

    def feed_near(k):
        farrive(k, here, z0 + k != z)
        for dev in (corner, px, py):
            fsend(k, dev)

    def feed_core(k):
        for place in (beside_at, across_at, corner_at):
            farrive(k, place)
        blocks = fbuf.at[k, c]
        send(blocks, blocks, fc_in + k, pc)

    def feed_forward(ks):
        if ks[0] == 0:
            load_g.wait()
            load_u.wait()
            load_d.wait()
        rows = slice(64 * ks[0], 64 * ks[-1] + 64)
        gate = up = None
        for h in range(2):
            for k in ks:
                if h == 0:
                    arrive(fbuf.at[k, 1 - c], fc_in + k)
                for p in range(4):
                    one, two = (fbuf[k, p // 2, 2 * (p % 2) + i, h].astype(f32) for i in range(2))
                    at = slice(64 * k + 16 * p, 64 * k + 16 * p + 16)
                    xq[0, at, :] = pack(one[:8], two[:8])
                    xq[1, at, :] = pack(one[8:], two[8:])
            for i in range(2):
                k_cols = cols(2 * h + i)
                gate_more = lax.dot_general(xq[i, rows, :], wg[:, k_cols], (((1,), (1,)), ((), ())), preferred_element_type=f32)
                up_more = lax.dot_general(xq[i, rows, :], wu[:, k_cols], (((1,), (1,)), ((), ())), preferred_element_type=f32)
                gate = gate_more if gate is None else gate + gate_more
                up = up_more if up is None else up + up_more
        bent = 0.5 * gate * (1.0 + jnp.tanh(math.sqrt(2.0 / math.pi) * (gate + 0.044715 * (gate * gate * gate))))
        hidden = (bent * up).astype(bf16)
        for h in range(2):
            for q in (2 * h, 2 * h + 1):
                part[q, rows, :] = jnp.dot(hidden, wd[:, cols(q)], preferred_element_type=f32)
            for k in ks:
                for place in range(4):
                    send_d0[h, k, place] = piece(h, k, 1 - c, place).astype(bf16)
                send(send_d0.at[h, k], recv_d0.at[h, k], d0_in + 3 * h + k, pc)

    def piece(h, k, core, place):
        rows = pl.ds(pl.multiple_of(64 * k + 32 * core + 8 * place, 8), 8)
        return jnp.concatenate([part[2 * h, rows, :], part[2 * h + 1, rows, :]], axis=0)

    def sum_core(k):
        for h in range(2):
            arrive(recv_d0.at[h, k], d0_in + 3 * h + k)
        for place, dev in ((corner_at, corner), (beside_at, px), (across_at, py), (here, None)):
            for h in range(2):
                v = piece(h, k, c, place) + recv_d0[h, k, place].astype(f32)
                if dev is None:
                    keep_d1[k, h] = v
                else:
                    send_d1[k, place, h] = v.astype(bf16)
            if dev is not None:
                send(send_d1.at[k, place], recv_d1.at[k, here], d1_in + 4 * k + here, dev)

    def sum_near(k):
        for place in (beside_at, across_at, corner_at):
            arrive(recv_d1.at[k, place], d1_in + 4 * k + place)
        mine = z0 + k == z
        for h in range(2):
            v = keep_d1[k, h]
            for place in (beside_at, across_at, corner_at):
                v = v + recv_d1[k, place, h].astype(f32)

            @pl.when(mine)
            def _():
                own_d[h] = v

            @pl.when(jnp.logical_not(mine))
            def _():
                send_d3[k, h] = v.astype(bf16)

        send(send_d3.at[k], recv_d3.at[z], d3_in + z, at_z(z0 + k), jnp.logical_not(mine))

    def rsend(t, dev, cond=None):
        send(rbuf.at[t], rbuf.at[t], rb_in + t, dev, cond)

    def finish(k):
        mine = z0 + k == z

        @pl.when(mine)
        def _():
            halves = [own_d[0], own_d[1]]
            for far in range(1, 4):
                src = (z + far) % 4
                arrive(recv_d3.at[src], d3_in + src)
                halves = [halves[h] + recv_d3[src, h].astype(f32) for h in range(2)]
            summed = [half[8 * i : 8 * i + 8] for half in halves for i in range(2)]
            scale = mean_scale(summed)
            res = [mid[q] + summed[q] * scale * g4_ref[cols(q)][None, :] for q in range(4)]
            for h in range(2):
                rbuf[3 * x + k, h] = pack(res[2 * h], res[2 * h + 1])

        for far in (2, 1, 3):
            rsend(3 * x + k, at_z((z + far) % 4), mine)

    def place_rows(t):
        for h in range(2):
            v = rbuf[t, h].astype(f32)
            for i in range(2):
                out_ref[2 * t, :, cols(2 * h + i)] = v[8 * i : 8 * i + 4].astype(bf16)
                out_ref[2 * t + 1, :, cols(2 * h + i)] = v[8 * i + 4 : 8 * i + 8].astype(bf16)

    def result_near(k):
        arrive(rbuf.at[3 * x + k], rb_in + 3 * x + k, z0 + k != z)
        rsend(3 * x + k, px)
        place_rows(3 * x + k)

    def result_far(k):
        arrive(rbuf.at[3 * (1 - x) + k], rb_in + 3 * (1 - x) + k)
        place_rows(3 * (1 - x) + k)

    for act, k in ((feed_near, 0), (feed_near, 1), (feed_near, 2), (feed_core, 0), (feed_core, 1), (feed_forward, (0,1,)), (feed_core, 2), (sum_core, 0), (sum_core, 1), (feed_forward, (2,)), (sum_core, 2), (sum_near, 0), (sum_near, 1), (sum_near, 2), (finish, 0), (finish, 1), (finish, 2), (result_near, 0), (result_near, 1), (result_near, 2), (result_far, 0), (result_far, 1), (result_far, 2)):
        act(k)

    for cond, copy in pending:
        when(cond, copy.wait_send)
    assert counts["send"] <= SENDS and counts["recv"] <= RECVS, counts


SENDS, RECVS, LOADS = 192, 192, 18


def grouped(
    embedded, cache_keys, cache_values, token_owner, dealing, lengths,
    project_weight, output_weight, gate_weight, up_weight, down_weight,
    gain_first, gain_second, gain_third, gain_fourth,
):
    f32, bf16 = jnp.float32, jnp.bfloat16
    width = embedded.shape[2]
    by_slot = embedded.transpose(1, 0, 2)
    gate_rows, up_rows = gate_weight.T, up_weight.T
    vmem = pl.BlockSpec(memory_space=pltpu.VMEM)
    hbm = pl.BlockSpec(memory_space=pl.ANY)
    V = pltpu.VMEM
    scratch = [
        pltpu.SMEM(dealing.shape, jnp.int32), pltpu.SMEM(lengths.shape, jnp.int32), V(token_owner.shape, jnp.int32),
        *[V(gain_first.shape, f32)] * 4, V(by_slot.shape, bf16),
        V((4, width, HD), bf16), V(cache_keys.shape[1:], bf16), V(cache_values.shape[1:], bf16),
        V(output_weight.shape, bf16), V(gate_rows.shape, bf16), V(up_rows.shape, bf16), V(down_weight.shape, bf16),
        V((48, width), f32), V((48, width), bf16), V((20, 48, HD), bf16), V((2, 48, HD), bf16),
        V((4, 96, HD), bf16), V((4, 96, HD), f32), V((4, 96, HD), bf16), V((4, 96, HD), bf16), V((4, 96, HD), bf16), V((96, HD), f32),
        V((8, 128), f32), V((8, 8, 128), f32), V((4, 48, 896), f32),
        V((2, 3, 16, 896), bf16), V((2, 3, 16, 896), bf16), V((2, 3, 16, 896), bf16), V((2, 4, 16, 896), bf16), V((2, 16, 896), f32), V((4, 8, 896), f32),
        V((3, 2, 4, 2, 16, 896), bf16), V((2, 192, 896), bf16), V((4, 192, 896), f32),
        V((2, 3, 4, 16, 896), bf16), V((2, 3, 4, 16, 896), bf16),
        V((3, 4, 2, 16, 896), bf16), V((3, 4, 2, 16, 896), bf16), V((3, 2, 16, 896), f32),
        V((3, 2, 16, 896), bf16), V((4, 2, 16, 896), bf16), V((2, 16, 896), f32), V((6, 2, 16, 896), bf16),
        pltpu.SemaphoreType.DMA((LOADS,)), pltpu.SemaphoreType.DMA((SENDS,)), pltpu.SemaphoreType.DMA((RECVS,)),
    ]
    results = pl.pallas_call(
        group_kernel,
        out_shape=jax.ShapeDtypeStruct(by_slot.shape, bf16),
        in_specs=[hbm] * 15,
        out_specs=vmem,
        scratch_shapes=scratch,
        name="decode_layer",
        compiler_params=pltpu.CompilerParams(collective_id=0, has_side_effects=True, vmem_limit_bytes=56 * 2**20),
    )(
        dealing, lengths, token_owner, gain_first, gain_second, gain_third, gain_fourth, by_slot,
        project_weight, cache_keys, cache_values, output_weight, gate_rows, up_rows, down_weight,
    )
    return results.transpose(1, 0, 2)


def solution(mesh):
    fits = mesh.shape["req"] == 4 and mesh.shape["seq"] == 8
    return jax.shard_map(
        grouped if fits else body,
        mesh=mesh,
        in_specs=(
            P(None, "req", None),
            P("req", "seq", None),
            P("req", "seq", None),
            P("req", "seq"),
            P(),
            P(),
            P(None, "seq"),
            P("seq", None),
            P(None, ("req", "seq")),
            P(None, ("req", "seq")),
            P(("req", "seq"), None),
            P(),
            P(),
            P(),
            P(),
        ),
        out_specs=P(None, "req", None),
        check_vma=False,
    )
```

```python
import math

import jax
import jax.numpy as jnp
from jax import lax
from jax.experimental import pallas as pl
from jax.experimental.pallas import tpu as pltpu
from jax.sharding import PartitionSpec as P

H = 16
KVH = 8
HD = 256
STEPS = 4
MESH = pl.DeviceIdType.MESH


soft_cap = 50.0
epsilon = 1e-06


def rms_scale(values, gain):
    mean_square = jnp.mean(values * values, axis=-1, keepdims=True)
    return values * lax.rsqrt(mean_square + epsilon) * gain


def rotate(values, positions):
    half_width = values.shape[-1] // 2
    freq_index = jnp.arange(half_width, dtype=jnp.float32)
    inverse = jnp.exp(freq_index * (-2.0 * math.log(10000.0) / values.shape[-1]))
    angles = positions[:, None] * inverse[None, :]
    cosine = jnp.cos(angles)[:, None, :]
    sine = jnp.sin(angles)[:, None, :]
    first_half = values[..., :half_width]
    second_half = values[..., half_width:]
    return jnp.concatenate(
        [first_half * cosine - second_half * sine, second_half * cosine + first_half * sine],
        axis=-1,
    )


def capped_weight(scores):
    return jnp.exp(soft_cap * jnp.tanh(scores / soft_cap))


def rounded(values):
    return lax.optimization_barrier(values.astype(jnp.bfloat16)).astype(jnp.float32)


def body(
    embedded,
    cache_keys,
    cache_values,
    token_owner,
    dealing,
    lengths,
    project_weight,
    output_weight,
    gate_weight,
    up_weight,
    down_weight,
    gain_first,
    gain_second,
    gain_third,
    gain_fourth,
):
    row_count = embedded.shape[1]
    rows = STEPS * row_count
    width = embedded.shape[2]
    local_tokens = cache_keys.shape[1]
    value_width = cache_keys.shape[2]
    group_size = H // KVH
    attention_width = H * HD
    column_count = output_weight.shape[0]
    group_index = lax.axis_index("req")
    seq_index = lax.axis_index("seq")
    seq_size = lax.axis_size("seq")
    req_size = lax.axis_size("req")
    column_start = seq_index * column_count
    slot_requests = lax.dynamic_slice_in_dim(dealing, group_index * row_count, row_count)
    matches = slot_requests[:, None] == jnp.arange(dealing.shape[0], dtype=jnp.int32)[None, :]
    base_positions = jnp.sum(jnp.where(matches, lengths[None, :], 0), axis=1)
    positions = base_positions[None, :] + jnp.arange(STEPS, dtype=jnp.int32)[:, None]
    positions = positions.reshape(rows).astype(jnp.float32)
    key_pool = cache_keys[0].reshape(local_tokens, KVH, HD)
    value_pool = cache_values[0].reshape(local_tokens, KVH, HD)
    slots = jnp.tile(jnp.arange(row_count, dtype=jnp.int32), STEPS)
    moments = jnp.repeat(jnp.arange(STEPS, dtype=jnp.int32), row_count)
    owned_mask = token_owner[0][None, :] == slots[:, None]
    stream = embedded.reshape(rows, width).astype(jnp.float32)
    normed = rms_scale(stream, gain_first).astype(jnp.bfloat16)
    local_part = jnp.dot(normed, project_weight, preferred_element_type=jnp.float32).astype(
        jnp.bfloat16
    )
    projected = lax.all_gather(local_part, "seq", axis=1, tiled=True)
    query_rows = projected[:, :attention_width].astype(jnp.float32).reshape(rows, H, HD)
    queries = (rotate(query_rows, positions) * HD ** (-0.5)).astype(jnp.bfloat16)
    key_rows = (
        projected[:, attention_width : attention_width + value_width]
        .astype(jnp.float32)
        .reshape(rows, KVH, HD)
    )
    fresh_keys = rotate(key_rows, positions).astype(jnp.bfloat16)
    fresh_values = projected[:, attention_width + value_width :].reshape(rows, KVH, HD)
    grouped = queries.reshape(rows, KVH, group_size, HD)
    all_keys = jnp.concatenate([key_pool, fresh_keys], axis=0)
    all_values = jnp.concatenate([value_pool, fresh_values], axis=0)
    fresh_mask = (
        (slots[None, :] == slots[:, None])
        & (moments[None, :] <= moments[:, None])
        & (seq_index == 0)
    )
    mask = jnp.concatenate([owned_mask, fresh_mask], axis=1)
    scores = jnp.einsum("igqd,tgd->igqt", grouped, all_keys, preferred_element_type=jnp.float32)
    weights = jnp.where(mask[:, None, None, :], capped_weight(scores), 0.0)
    totals = lax.psum(jnp.sum(weights, axis=-1), "seq").reshape(rows, H)
    outputs = jnp.einsum(
        "igqt,tgd->igqd",
        weights.astype(jnp.bfloat16),
        all_values,
        preferred_element_type=jnp.float32,
    ).reshape(rows, attention_width)
    outputs = lax.psum_scatter(outputs, "seq", scatter_dimension=1, tiled=True)
    spread = jnp.repeat(totals, HD, axis=1)
    spread = lax.dynamic_slice_in_dim(spread, column_start, column_count, 1)
    attended = (outputs / spread).astype(jnp.bfloat16)
    partial = jnp.dot(attended, output_weight, preferred_element_type=jnp.float32)
    mixed = lax.psum(partial, "seq")
    middle = stream + rms_scale(mixed, gain_second)
    feed_input = rms_scale(middle, gain_third).astype(jnp.bfloat16)
    block_rows = lax.all_gather(feed_input, "req", axis=0, tiled=True)
    gate_part = jnp.dot(block_rows, gate_weight, preferred_element_type=jnp.float32)
    up_part = jnp.dot(block_rows, up_weight, preferred_element_type=jnp.float32)
    hidden = (jax.nn.gelu(gate_part, approximate=True) * up_part).astype(jnp.bfloat16)
    summed = jnp.dot(hidden, down_weight, preferred_element_type=jnp.float32)
    summed = lax.psum_scatter(summed, "req", scatter_dimension=0, tiled=True)
    summed = lax.psum(summed, "seq")
    results = (middle + rms_scale(summed, gain_fourth)).astype(jnp.bfloat16)
    return results.reshape(STEPS, row_count, width)


def group_kernel(
    dealing_hbm, lengths_hbm, owner_hbm, g1_hbm, g2_hbm, g3_hbm, g4_hbm, emb_hbm,
    wp_hbm, kc_hbm, vc_hbm, wo_hbm, wg_hbm, wu_hbm, wd_hbm,
    out_ref,
    dealing_ref, lengths_ref, owner_ref, g1_ref, g2_ref, g3_ref, g4_ref, emb_ref,
    wp, kc, vc, wo, wg, wu, wd,
    rows32, normed, qall, fresh, obuf, keep_b, recv_bx, send_bz, recv_bz, own_b,
    send_t, recv_t, mix32, send_cx, recv_cx, send_cz, recv_cz, own_c, mid,
    fbuf, xq, part, send_d0, recv_d0, send_d1, recv_d1, keep_d1, send_d3, recv_d3, own_d, rbuf,
    load_sem, send_sem, recv_sem,
):
    f32, bf16 = jnp.float32, jnp.bfloat16
    r, s = lax.axis_index("req"), lax.axis_index("seq")
    y, c = r // 2, r % 2
    z, x = s // 2, s % 2
    px, py, pc = (r, z * 2 + 1 - x), ((1 - y) * 2 + c, s), (y * 2 + 1 - c, s)

    def at_z(other):
        return (r, other * 2 + x)

    barrier = pltpu.get_barrier_semaphore()
    partners = [(r, (s + k) % 8) for k in range(1, 8)] + [py, pc]
    for partner in partners:
        pl.semaphore_signal(barrier, inc=1, device_id=partner, device_id_type=MESH)

    loads = []

    def load(src, dst):
        copy = pltpu.make_async_copy(src, dst, load_sem.at[len(loads)])
        copy.start()
        loads.append(copy)
        return copy

    small = [
        load(emb_hbm, emb_ref), load(g1_hbm, g1_ref), load(dealing_hbm, dealing_ref), load(lengths_hbm, lengths_ref),
        load(owner_hbm, owner_ref), load(g2_hbm, g2_ref), load(g3_hbm, g3_ref), load(g4_hbm, g4_ref),
    ]
    load_p = [load(wp_hbm.at[896 * j : 896 * j + 896, :], wp.at[896 * j : 896 * j + 896, :]) for j in range(4)]

    counts = {"send": 0, "recv": 0}
    pending = []

    def slots(n):
        base = counts["recv"]
        counts["recv"] += n
        return base

    def send(src, dst, rid, dev, cond=None):
        sid = counts["send"]
        counts["send"] += 1
        copy = pltpu.make_async_remote_copy(
            src_ref=src, dst_ref=dst, send_sem=send_sem.at[sid], recv_sem=recv_sem.at[rid],
            device_id=dev, device_id_type=MESH,
        )
        when(cond, copy.start)
        pending.append((cond, copy))

    def when(cond, fn):
        if cond is None:
            fn()
        else:
            pl.when(cond)(fn)

    def arrive(dst, rid, cond=None):
        copy = pltpu.make_async_remote_copy(
            src_ref=dst, dst_ref=dst, send_sem=send_sem.at[0], recv_sem=recv_sem.at[rid],
            device_id=px, device_id_type=MESH,
        )
        when(cond, copy.wait_recv)

    def pack(top, bottom):
        return jnp.concatenate([top, bottom], axis=0).astype(bf16)

    for copy in small:
        copy.wait()
    for t in range(6):
        rows32[8 * t : 8 * t + 8, :] = jnp.concatenate([emb_ref[2 * t].astype(f32), emb_ref[2 * t + 1].astype(f32)], axis=0)
    gain = g1_ref[...][None, :]
    for t in range(3):
        v = rows32[16 * t : 16 * t + 16, :]
        scale = lax.rsqrt(jnp.mean(v * v, axis=-1, keepdims=True) + epsilon)
        normed[16 * t : 16 * t + 16, :] = (v * scale * gain).astype(bf16)

    row = lax.broadcasted_iota(jnp.int32, (48, 128), 0)
    position = row % STEPS
    for i in range(12):
        position = position + jnp.where(row // STEPS == i, lengths_ref[dealing_ref[12 * r + i]], 0)
    lane = lax.broadcasted_iota(jnp.int32, (48, 128), 1).astype(f32)
    angles = position.astype(f32) * jnp.exp(lane * (-2.0 * math.log(10000.0) / HD))
    cosine, sine = jnp.cos(angles), jnp.sin(angles)

    base = jnp.where(s < 4, 4 * s, 16)
    is_query = z < 2
    value_role = z == 3
    cosv = jnp.where(value_role, 1.0, cosine)
    sinv = jnp.where(value_role, 0.0, sine)
    factor = jnp.where(is_query, HD ** (-0.5), 1.0)
    q_in, f_in = slots(16), slots(2)
    kv = jnp.maximum(z - 2, 0)
    heads = None
    for j in range(4):
        load_p[j].wait()
        if j == 2:
            load_k = load(kc_hbm.at[0], kc)
            load_v = load(vc_hbm.at[0], vc)
            load_o = load(wo_hbm, wo)
            load_g = load(wg_hbm, wg)
            load_u = load(wu_hbm, wu)
            load_d = load(wd_hbm, wd)
        k_rows = slice(896 * j, 896 * j + 896)
        more = jnp.dot(normed[:, k_rows], wp[k_rows, :], preferred_element_type=f32)
        heads = more if heads is None else heads + more
    for j in range(4):
        proj = heads[:, HD * j : HD * j + HD].astype(bf16).astype(f32)
        a, b = proj[:, :128], proj[:, 128:]
        turned = jnp.concatenate([a * cosv - b * sinv, b * cosv + a * sinv], axis=1)
        qall[base + j] = (turned * factor).astype(bf16)
    pl.semaphore_wait(barrier, len(partners))
    for j in range(4):
        head = qall.at[base + j]
        rid = q_in + jnp.minimum(base + j, 15)
        qdst = qall.at[jnp.minimum(base + j, 15)]
        send(head, qdst, rid, at_z(2), is_query)
        send(head, qdst, rid, at_z(1 - jnp.minimum(z, 1)), is_query)
        send(head, qdst, rid, px, is_query)
        e = 4 * x + j
        send(head, fresh.at[kv], f_in + kv, (r, e), (z >= 2) & (e != s))

        @pl.when((z >= 2) & (e == s))
        def _():
            fresh[kv] = qall[base + j]

    for j in range(4):
        for a in range(2):
            h = 8 * a + 4 * x + j
            arrive(qall.at[h], q_in + h, z != a)
            send(qall.at[h], qall.at[h], q_in + h, at_z(3), z == 2)
            send(qall.at[h], qall.at[h], q_in + h, px, z != a)

    row_slot = (lax.broadcasted_iota(jnp.int32, (96, 1), 0) % 48) // STEPS
    owned = owner_ref[...] == row_slot
    eye = lax.broadcasted_iota(jnp.int32, (96, 128), 0) == lax.broadcasted_iota(jnp.int32, (96, 128), 1)
    table_row = lax.broadcasted_iota(jnp.int32, (8, 128), 0)
    table = jnp.zeros((8, 128), f32)
    bx_in = slots(4)
    load_k.wait()
    load_v.wait()
    for column in range(2):
        cx = x if column == 0 else 1 - x
        if column == 1:
            for j in range(4):
                for a in range(2):
                    h = 8 * a + 4 * cx + j
                    arrive(qall.at[h], q_in + h)
        for away in range(2):
            jj = 1 - x if away == 0 else x
            for a in range(2):
                e = 4 * a + 2 * cx + jj
                zd = e // 2
                lanes = pl.ds(pl.multiple_of(e * HD, HD), HD)
                qe = qall[pl.ds(2 * e, 2)].reshape(96, HD)
                scores = lax.dot_general(qe, kc[:, lanes], (((1,), (1,)), ((), ())), preferred_element_type=f32)
                w = jnp.where(owned, capped_weight(scores), 0.0)
                total = jnp.sum(w, axis=-1, keepdims=True)
                line = jnp.sum(jnp.where(eye, total, 0.0), axis=0, keepdims=True)
                table = jnp.where(table_row == e, line, table)
                o = jnp.dot(w.astype(bf16), vc[:, lanes], preferred_element_type=f32)
                if away == 0:
                    obuf[zd] = o.astype(bf16)
                    send(obuf.at[zd], recv_bx.at[zd], bx_in + zd, px)
                else:
                    keep_b[zd] = o
    t_in = slots(8)
    send_t[...] = table
    for k in range(1, 8):
        send(send_t, recv_t.at[s], t_in + s, (r, (s + k) % 8))

    bz_in = slots(4)
    for first in (1 - x, x):
        for a in range(2):
            zd = 2 * a + first
            arrive(recv_bx.at[zd], bx_in + zd)
            v = keep_b[zd] + recv_bx[zd].astype(f32)

            @pl.when(zd == z)
            def _():
                own_b[...] = v

            @pl.when(zd != z)
            def _():
                send_bz[zd] = v.astype(bf16)

            send(send_bz.at[zd], recv_bz.at[z], bz_in + z, at_z(zd), zd != z)

    arrive(fresh.at[0], f_in, 4 + s // 4 != s)
    arrive(fresh.at[1], f_in + 1, 6 + s // 4 != s)
    qe = qall[pl.ds(2 * s, 2)].reshape(96, HD)
    scores = lax.dot_general(qe, fresh[0], (((1,), (1,)), ((), ())), preferred_element_type=f32)
    ri = lax.broadcasted_iota(jnp.int32, (96, 48), 0) % 48
    ci = lax.broadcasted_iota(jnp.int32, (96, 48), 1)
    seen = (ri // STEPS == ci // STEPS) & (ci % STEPS <= ri % STEPS)
    w = jnp.where(seen, capped_weight(scores), 0.0)
    totals = jnp.sum(w, axis=-1, keepdims=True)
    fresh_out = jnp.dot(w.astype(bf16), fresh[1], preferred_element_type=f32)

    for k in range(1, 8):
        src = (s + k) % 8
        arrive(recv_t.at[src], t_in + src)
        table = table + recv_t[src]
    line = jnp.sum(jnp.where(table_row == s, table, 0.0), axis=0, keepdims=True)
    totals = totals + jnp.sum(jnp.where(eye, line, 0.0), axis=-1, keepdims=True)
    outs = fresh_out + own_b[...]
    for k in range(1, 4):
        src = (z + k) % 4
        arrive(recv_bz.at[src], bz_in + src)
        outs = outs + recv_bz[src].astype(f32)
    attended = outs / totals
    attended = jnp.concatenate([attended[:48], attended[48:]], axis=1).astype(bf16)

    z0 = (x + c) % 2
    k_me = z - z0
    is_owner = (k_me >= 0) & (k_me <= 2)
    cx_in, cz_in = slots(2), slots(8)
    load_o.wait()
    for h in range(2):
        for q in (2 * h, 2 * h + 1):
            mix32[q] = jnp.dot(attended, wo[:, 896 * q : 896 * q + 896], preferred_element_type=f32)

        def tile(k, col):
            rows = pl.ds(pl.multiple_of(24 * col + 8 * k, 8), 8)
            return mix32[2 * h, rows, :], mix32[2 * h + 1, rows, :]

        for k in range(3):
            send_cx[h, k] = pack(*tile(k, 1 - x))
        send(send_cx.at[h], recv_cx.at[h], cx_in + h, px)
    for h in range(2):
        arrive(recv_cx.at[h], cx_in + h)
        for k in range(3):
            rows = pl.ds(pl.multiple_of(24 * x + 8 * k, 8), 8)
            v = jnp.concatenate([mix32[2 * h, rows, :], mix32[2 * h + 1, rows, :]], axis=0)
            v = v + recv_cx[h, k].astype(f32)

            @pl.when(z0 + k == z)
            def _():
                own_c[h] = v

            @pl.when(z0 + k != z)
            def _():
                send_cz[h, k] = v.astype(bf16)

            send(send_cz.at[h, k], recv_cz.at[h, z], cz_in + 4 * h + z, at_z(z0 + k), z0 + k != z)

    my_rows = pl.ds(pl.multiple_of(24 * x + 8 * jnp.clip(k_me, 0, 2), 8), 8)
    k_own = jnp.clip(k_me, 0, 2)
    here = 2 * y + x

    def quarters(buf, recv, rid):
        out = []
        for h in range(2):
            v = buf[h]
            for k in range(1, 4):
                src = (z + k) % 4
                arrive(recv.at[h, src], rid + 4 * h + src)
                v = v + recv[h, src].astype(f32)
            out += [v[:8], v[8:]]
        return out

    def mean_scale(parts):
        square = sum(jnp.sum(p * p, axis=-1, keepdims=True) for p in parts)
        return lax.rsqrt(square * (1.0 / 3584.0) + epsilon)

    def cols(q):
        return slice(896 * q, 896 * q + 896)

    @pl.when(is_owner)
    def _():
        mixed = quarters(own_c, recv_cz, cz_in)
        scale = mean_scale(mixed)
        middle = [rows32[my_rows, cols(q)] + mixed[q] * scale * g2_ref[cols(q)][None, :] for q in range(4)]
        scale = mean_scale(middle)
        for q in range(4):
            mid[q] = middle[q]
        feed = [middle[q] * scale * g3_ref[cols(q)][None, :] for q in range(4)]
        for h in range(2):
            fbuf[k_own, c, here, h] = pack(feed[2 * h], feed[2 * h + 1])

    fb_in, fc_in = slots(12), slots(3)
    d0_in, d1_in, d3_in, rb_in = slots(6), slots(12), slots(4), slots(6)
    corner = ((1 - y) * 2 + c, z * 2 + 1 - x)
    beside_at, across_at, corner_at = 2 * y + 1 - x, 2 * (1 - y) + x, 2 * (1 - y) + 1 - x

    def fsend(k, dev, cond=None):
        block = fbuf.at[k, c, here]
        send(block, block, fb_in + 4 * k + here, dev, cond)

    def farrive(k, place, cond=None):
        arrive(fbuf.at[k, c, place], fb_in + 4 * k + place, cond)

    for far in (1, 2, 3):
        fsend(k_own, at_z((z + far) % 4), is_owner)

    def feed_near(k):
        farrive(k, here, z0 + k != z)
        for dev in (corner, px, py):
            fsend(k, dev)

    def feed_core(k):
        for place in (beside_at, across_at, corner_at):
            farrive(k, place)
        blocks = fbuf.at[k, c]
        send(blocks, blocks, fc_in + k, pc)

    def feed_forward(ks):
        if ks[0] == 0:
            load_g.wait()
            load_u.wait()
            load_d.wait()
        rows = slice(64 * ks[0], 64 * ks[-1] + 64)
        gate = up = None
        for h in range(2):
            for k in ks:
                if h == 0:
                    arrive(fbuf.at[k, 1 - c], fc_in + k)
                for p in range(4):
                    one, two = (fbuf[k, p // 2, 2 * (p % 2) + i, h].astype(f32) for i in range(2))
                    at = slice(64 * k + 16 * p, 64 * k + 16 * p + 16)
                    xq[0, at, :] = pack(one[:8], two[:8])
                    xq[1, at, :] = pack(one[8:], two[8:])
            for i in range(2):
                k_cols = cols(2 * h + i)
                gate_more = lax.dot_general(xq[i, rows, :], wg[:, k_cols], (((1,), (1,)), ((), ())), preferred_element_type=f32)
                up_more = lax.dot_general(xq[i, rows, :], wu[:, k_cols], (((1,), (1,)), ((), ())), preferred_element_type=f32)
                gate = gate_more if gate is None else gate + gate_more
                up = up_more if up is None else up + up_more
        bent = 0.5 * gate * (1.0 + jnp.tanh(math.sqrt(2.0 / math.pi) * (gate + 0.044715 * (gate * gate * gate))))
        hidden = (bent * up).astype(bf16)
        for h in range(2):
            for q in (2 * h, 2 * h + 1):
                part[q, rows, :] = jnp.dot(hidden, wd[:, cols(q)], preferred_element_type=f32)
            for k in ks:
                for place in range(4):
                    send_d0[h, k, place] = piece(h, k, 1 - c, place).astype(bf16)
                send(send_d0.at[h, k], recv_d0.at[h, k], d0_in + 3 * h + k, pc)

    def piece(h, k, core, place):
        rows = pl.ds(pl.multiple_of(64 * k + 32 * core + 8 * place, 8), 8)
        return jnp.concatenate([part[2 * h, rows, :], part[2 * h + 1, rows, :]], axis=0)

    def sum_core(k):
        for h in range(2):
            arrive(recv_d0.at[h, k], d0_in + 3 * h + k)
        for place, dev in ((corner_at, corner), (beside_at, px), (across_at, py), (here, None)):
            for h in range(2):
                v = piece(h, k, c, place) + recv_d0[h, k, place].astype(f32)
                if dev is None:
                    keep_d1[k, h] = v
                else:
                    send_d1[k, place, h] = v.astype(bf16)
            if dev is not None:
                send(send_d1.at[k, place], recv_d1.at[k, here], d1_in + 4 * k + here, dev)

    def sum_near(k):
        for place in (beside_at, across_at, corner_at):
            arrive(recv_d1.at[k, place], d1_in + 4 * k + place)
        mine = z0 + k == z
        for h in range(2):
            v = keep_d1[k, h]
            for place in (beside_at, across_at, corner_at):
                v = v + recv_d1[k, place, h].astype(f32)

            @pl.when(mine)
            def _():
                own_d[h] = v

            @pl.when(jnp.logical_not(mine))
            def _():
                send_d3[k, h] = v.astype(bf16)

        send(send_d3.at[k], recv_d3.at[z], d3_in + z, at_z(z0 + k), jnp.logical_not(mine))

    def rsend(t, dev, cond=None):
        send(rbuf.at[t], rbuf.at[t], rb_in + t, dev, cond)

    def finish(k):
        mine = z0 + k == z

        @pl.when(mine)
        def _():
            halves = [own_d[0], own_d[1]]
            for far in range(1, 4):
                src = (z + far) % 4
                arrive(recv_d3.at[src], d3_in + src)
                halves = [halves[h] + recv_d3[src, h].astype(f32) for h in range(2)]
            summed = [half[8 * i : 8 * i + 8] for half in halves for i in range(2)]
            scale = mean_scale(summed)
            res = [mid[q] + summed[q] * scale * g4_ref[cols(q)][None, :] for q in range(4)]
            for h in range(2):
                rbuf[3 * x + k, h] = pack(res[2 * h], res[2 * h + 1])

        for far in (1, 2, 3):
            rsend(3 * x + k, at_z((z + far) % 4), mine)

    def place_rows(t):
        for h in range(2):
            v = rbuf[t, h].astype(f32)
            for i in range(2):
                out_ref[2 * t, :, cols(2 * h + i)] = v[8 * i : 8 * i + 4].astype(bf16)
                out_ref[2 * t + 1, :, cols(2 * h + i)] = v[8 * i + 4 : 8 * i + 8].astype(bf16)

    def result_near(k):
        arrive(rbuf.at[3 * x + k], rb_in + 3 * x + k, z0 + k != z)
        rsend(3 * x + k, px)
        place_rows(3 * x + k)

    def result_far(k):
        arrive(rbuf.at[3 * (1 - x) + k], rb_in + 3 * (1 - x) + k)
        place_rows(3 * (1 - x) + k)

    for act, k in ((feed_near, 0), (feed_near, 1), (feed_near, 2), (feed_core, 0), (feed_core, 1), (feed_forward, (0,1,)), (feed_core, 2), (sum_core, 0), (sum_core, 1), (feed_forward, (2,)), (sum_core, 2), (sum_near, 0), (sum_near, 1), (sum_near, 2), (finish, 0), (finish, 1), (finish, 2), (result_near, 0), (result_near, 1), (result_near, 2), (result_far, 0), (result_far, 1), (result_far, 2)):
        act(k)

    for cond, copy in pending:
        when(cond, copy.wait_send)
    assert counts["send"] <= SENDS and counts["recv"] <= RECVS, counts


SENDS, RECVS, LOADS = 192, 192, 18


def grouped(
    embedded, cache_keys, cache_values, token_owner, dealing, lengths,
    project_weight, output_weight, gate_weight, up_weight, down_weight,
    gain_first, gain_second, gain_third, gain_fourth,
):
    f32, bf16 = jnp.float32, jnp.bfloat16
    width = embedded.shape[2]
    by_slot = embedded.transpose(1, 0, 2)
    gate_rows, up_rows = gate_weight.T, up_weight.T
    vmem = pl.BlockSpec(memory_space=pltpu.VMEM)
    hbm = pl.BlockSpec(memory_space=pl.ANY)
    V = pltpu.VMEM
    scratch = [
        pltpu.SMEM(dealing.shape, jnp.int32), pltpu.SMEM(lengths.shape, jnp.int32), V(token_owner.shape, jnp.int32),
        *[V(gain_first.shape, f32)] * 4, V(by_slot.shape, bf16),
        V(project_weight.shape, bf16), V(cache_keys.shape[1:], bf16), V(cache_values.shape[1:], bf16),
        V(output_weight.shape, bf16), V(gate_rows.shape, bf16), V(up_rows.shape, bf16), V(down_weight.shape, bf16),
        V((48, width), f32), V((48, width), bf16), V((20, 48, HD), bf16), V((2, 48, HD), bf16),
        V((4, 96, HD), bf16), V((4, 96, HD), f32), V((4, 96, HD), bf16), V((4, 96, HD), bf16), V((4, 96, HD), bf16), V((96, HD), f32),
        V((8, 128), f32), V((8, 8, 128), f32), V((4, 48, 896), f32),
        V((2, 3, 16, 896), bf16), V((2, 3, 16, 896), bf16), V((2, 3, 16, 896), bf16), V((2, 4, 16, 896), bf16), V((2, 16, 896), f32), V((4, 8, 896), f32),
        V((3, 2, 4, 2, 16, 896), bf16), V((2, 192, 896), bf16), V((4, 192, 896), f32),
        V((2, 3, 4, 16, 896), bf16), V((2, 3, 4, 16, 896), bf16),
        V((3, 4, 2, 16, 896), bf16), V((3, 4, 2, 16, 896), bf16), V((3, 2, 16, 896), f32),
        V((3, 2, 16, 896), bf16), V((4, 2, 16, 896), bf16), V((2, 16, 896), f32), V((6, 2, 16, 896), bf16),
        pltpu.SemaphoreType.DMA((LOADS,)), pltpu.SemaphoreType.DMA((SENDS,)), pltpu.SemaphoreType.DMA((RECVS,)),
    ]
    results = pl.pallas_call(
        group_kernel,
        out_shape=jax.ShapeDtypeStruct(by_slot.shape, bf16),
        in_specs=[hbm] * 15,
        out_specs=vmem,
        scratch_shapes=scratch,
        name="decode_layer",
        compiler_params=pltpu.CompilerParams(collective_id=0, has_side_effects=True, vmem_limit_bytes=56 * 2**20),
    )(
        dealing, lengths, token_owner, gain_first, gain_second, gain_third, gain_fourth, by_slot,
        project_weight, cache_keys, cache_values, output_weight, gate_rows, up_rows, down_weight,
    )
    return results.transpose(1, 0, 2)


def solution(mesh):
    fits = mesh.shape["req"] == 4 and mesh.shape["seq"] == 8
    return jax.shard_map(
        grouped if fits else body,
        mesh=mesh,
        in_specs=(
            P(None, "req", None),
            P("req", "seq", None),
            P("req", "seq", None),
            P("req", "seq"),
            P(),
            P(),
            P(None, "seq"),
            P("seq", None),
            P(None, ("req", "seq")),
            P(None, ("req", "seq")),
            P(("req", "seq"), None),
            P(),
            P(),
            P(),
            P(),
        ),
        out_specs=P(None, "req", None),
        check_vma=False,
    )
```

```python
import math

import jax
import jax.numpy as jnp
from jax import lax
from jax.experimental import pallas as pl
from jax.experimental.pallas import tpu as pltpu
from jax.sharding import PartitionSpec as P

H = 16
KVH = 8
HD = 256
STEPS = 4
MESH = pl.DeviceIdType.MESH


soft_cap = 50.0
epsilon = 1e-06


def rms_scale(values, gain):
    mean_square = jnp.mean(values * values, axis=-1, keepdims=True)
    return values * lax.rsqrt(mean_square + epsilon) * gain


def rotate(values, positions):
    half_width = values.shape[-1] // 2
    freq_index = jnp.arange(half_width, dtype=jnp.float32)
    inverse = jnp.exp(freq_index * (-2.0 * math.log(10000.0) / values.shape[-1]))
    angles = positions[:, None] * inverse[None, :]
    cosine = jnp.cos(angles)[:, None, :]
    sine = jnp.sin(angles)[:, None, :]
    first_half = values[..., :half_width]
    second_half = values[..., half_width:]
    return jnp.concatenate(
        [first_half * cosine - second_half * sine, second_half * cosine + first_half * sine],
        axis=-1,
    )


def capped_weight(scores):
    return jnp.exp(soft_cap * jnp.tanh(scores / soft_cap))


def rounded(values):
    return lax.optimization_barrier(values.astype(jnp.bfloat16)).astype(jnp.float32)


def body(
    embedded,
    cache_keys,
    cache_values,
    token_owner,
    dealing,
    lengths,
    project_weight,
    output_weight,
    gate_weight,
    up_weight,
    down_weight,
    gain_first,
    gain_second,
    gain_third,
    gain_fourth,
):
    row_count = embedded.shape[1]
    rows = STEPS * row_count
    width = embedded.shape[2]
    local_tokens = cache_keys.shape[1]
    value_width = cache_keys.shape[2]
    group_size = H // KVH
    attention_width = H * HD
    column_count = output_weight.shape[0]
    group_index = lax.axis_index("req")
    seq_index = lax.axis_index("seq")
    seq_size = lax.axis_size("seq")
    req_size = lax.axis_size("req")
    column_start = seq_index * column_count
    slot_requests = lax.dynamic_slice_in_dim(dealing, group_index * row_count, row_count)
    matches = slot_requests[:, None] == jnp.arange(dealing.shape[0], dtype=jnp.int32)[None, :]
    base_positions = jnp.sum(jnp.where(matches, lengths[None, :], 0), axis=1)
    positions = base_positions[None, :] + jnp.arange(STEPS, dtype=jnp.int32)[:, None]
    positions = positions.reshape(rows).astype(jnp.float32)
    key_pool = cache_keys[0].reshape(local_tokens, KVH, HD)
    value_pool = cache_values[0].reshape(local_tokens, KVH, HD)
    slots = jnp.tile(jnp.arange(row_count, dtype=jnp.int32), STEPS)
    moments = jnp.repeat(jnp.arange(STEPS, dtype=jnp.int32), row_count)
    owned_mask = token_owner[0][None, :] == slots[:, None]
    stream = embedded.reshape(rows, width).astype(jnp.float32)
    normed = rms_scale(stream, gain_first).astype(jnp.bfloat16)
    local_part = jnp.dot(normed, project_weight, preferred_element_type=jnp.float32).astype(
        jnp.bfloat16
    )
    projected = lax.all_gather(local_part, "seq", axis=1, tiled=True)
    query_rows = projected[:, :attention_width].astype(jnp.float32).reshape(rows, H, HD)
    queries = (rotate(query_rows, positions) * HD ** (-0.5)).astype(jnp.bfloat16)
    key_rows = (
        projected[:, attention_width : attention_width + value_width]
        .astype(jnp.float32)
        .reshape(rows, KVH, HD)
    )
    fresh_keys = rotate(key_rows, positions).astype(jnp.bfloat16)
    fresh_values = projected[:, attention_width + value_width :].reshape(rows, KVH, HD)
    grouped = queries.reshape(rows, KVH, group_size, HD)
    all_keys = jnp.concatenate([key_pool, fresh_keys], axis=0)
    all_values = jnp.concatenate([value_pool, fresh_values], axis=0)
    fresh_mask = (
        (slots[None, :] == slots[:, None])
        & (moments[None, :] <= moments[:, None])
        & (seq_index == 0)
    )
    mask = jnp.concatenate([owned_mask, fresh_mask], axis=1)
    scores = jnp.einsum("igqd,tgd->igqt", grouped, all_keys, preferred_element_type=jnp.float32)
    weights = jnp.where(mask[:, None, None, :], capped_weight(scores), 0.0)
    totals = lax.psum(jnp.sum(weights, axis=-1), "seq").reshape(rows, H)
    outputs = jnp.einsum(
        "igqt,tgd->igqd",
        weights.astype(jnp.bfloat16),
        all_values,
        preferred_element_type=jnp.float32,
    ).reshape(rows, attention_width)
    outputs = lax.psum_scatter(outputs, "seq", scatter_dimension=1, tiled=True)
    spread = jnp.repeat(totals, HD, axis=1)
    spread = lax.dynamic_slice_in_dim(spread, column_start, column_count, 1)
    attended = (outputs / spread).astype(jnp.bfloat16)
    partial = jnp.dot(attended, output_weight, preferred_element_type=jnp.float32)
    mixed = lax.psum(partial, "seq")
    middle = stream + rms_scale(mixed, gain_second)
    feed_input = rms_scale(middle, gain_third).astype(jnp.bfloat16)
    block_rows = lax.all_gather(feed_input, "req", axis=0, tiled=True)
    gate_part = jnp.dot(block_rows, gate_weight, preferred_element_type=jnp.float32)
    up_part = jnp.dot(block_rows, up_weight, preferred_element_type=jnp.float32)
    hidden = (jax.nn.gelu(gate_part, approximate=True) * up_part).astype(jnp.bfloat16)
    summed = jnp.dot(hidden, down_weight, preferred_element_type=jnp.float32)
    summed = lax.psum_scatter(summed, "req", scatter_dimension=0, tiled=True)
    summed = lax.psum(summed, "seq")
    results = (middle + rms_scale(summed, gain_fourth)).astype(jnp.bfloat16)
    return results.reshape(STEPS, row_count, width)


def group_kernel(
    dealing_hbm, lengths_hbm, owner_hbm, g1_hbm, g2_hbm, g3_hbm, g4_hbm, emb_hbm,
    wp_hbm, kc_hbm, vc_hbm, wo_hbm, wg_hbm, wu_hbm, wd_hbm,
    out_ref,
    dealing_ref, lengths_ref, owner_ref, g1_ref, g2_ref, g3_ref, g4_ref, emb_ref,
    wp, kc, vc, wo, wg, wu, wd,
    rows32, normed, qall, fresh, obuf, keep_b, recv_bx, send_bz, recv_bz, own_b,
    send_t, recv_t, mix32, send_cx, recv_cx, send_cz, recv_cz, own_c, mid,
    fbuf, xq, part, send_d0, recv_d0, send_d1, recv_d1, keep_d1, send_d3, recv_d3, own_d, rbuf,
    load_sem, send_sem, recv_sem,
):
    f32, bf16 = jnp.float32, jnp.bfloat16
    r, s = lax.axis_index("req"), lax.axis_index("seq")
    y, c = r // 2, r % 2
    z, x = s // 2, s % 2
    px, py, pc = (r, z * 2 + 1 - x), ((1 - y) * 2 + c, s), (y * 2 + 1 - c, s)

    def at_z(other):
        return (r, other * 2 + x)

    barrier = pltpu.get_barrier_semaphore()
    partners = [(r, (s + k) % 8) for k in range(1, 8)] + [py, pc]
    for partner in partners:
        pl.semaphore_signal(barrier, inc=1, device_id=partner, device_id_type=MESH)

    loads = []

    def load(src, dst):
        copy = pltpu.make_async_copy(src, dst, load_sem.at[len(loads)])
        copy.start()
        loads.append(copy)
        return copy

    small = [
        load(emb_hbm, emb_ref), load(g1_hbm, g1_ref), load(dealing_hbm, dealing_ref), load(lengths_hbm, lengths_ref),
        load(owner_hbm, owner_ref), load(g2_hbm, g2_ref), load(g3_hbm, g3_ref), load(g4_hbm, g4_ref),
    ]
    load_p = [load(wp_hbm.at[896 * j : 896 * j + 896, :], wp.at[896 * j : 896 * j + 896, :]) for j in range(4)]

    counts = {"send": 0, "recv": 0}
    pending = []

    def slots(n):
        base = counts["recv"]
        counts["recv"] += n
        return base

    def send(src, dst, rid, dev, cond=None):
        sid = counts["send"]
        counts["send"] += 1
        copy = pltpu.make_async_remote_copy(
            src_ref=src, dst_ref=dst, send_sem=send_sem.at[sid], recv_sem=recv_sem.at[rid],
            device_id=dev, device_id_type=MESH,
        )
        when(cond, copy.start)
        pending.append((cond, copy))

    def when(cond, fn):
        if cond is None:
            fn()
        else:
            pl.when(cond)(fn)

    def arrive(dst, rid, cond=None):
        copy = pltpu.make_async_remote_copy(
            src_ref=dst, dst_ref=dst, send_sem=send_sem.at[0], recv_sem=recv_sem.at[rid],
            device_id=px, device_id_type=MESH,
        )
        when(cond, copy.wait_recv)

    def pack(top, bottom):
        return jnp.concatenate([top, bottom], axis=0).astype(bf16)

    for copy in small:
        copy.wait()
    for t in range(6):
        rows32[8 * t : 8 * t + 8, :] = jnp.concatenate([emb_ref[2 * t].astype(f32), emb_ref[2 * t + 1].astype(f32)], axis=0)
    gain = g1_ref[...][None, :]
    for t in range(3):
        v = rows32[16 * t : 16 * t + 16, :]
        scale = lax.rsqrt(jnp.mean(v * v, axis=-1, keepdims=True) + epsilon)
        normed[16 * t : 16 * t + 16, :] = (v * scale * gain).astype(bf16)

    row = lax.broadcasted_iota(jnp.int32, (48, 128), 0)
    position = row % STEPS
    for i in range(12):
        position = position + jnp.where(row // STEPS == i, lengths_ref[dealing_ref[12 * r + i]], 0)
    lane = lax.broadcasted_iota(jnp.int32, (48, 128), 1).astype(f32)
    angles = position.astype(f32) * jnp.exp(lane * (-2.0 * math.log(10000.0) / HD))
    cosine, sine = jnp.cos(angles), jnp.sin(angles)

    base = jnp.where(s < 4, 4 * s, 16)
    is_query = z < 2
    value_role = z == 3
    cosv = jnp.where(value_role, 1.0, cosine)
    sinv = jnp.where(value_role, 0.0, sine)
    factor = jnp.where(is_query, HD ** (-0.5), 1.0)
    q_in, f_in = slots(16), slots(2)
    kv = jnp.maximum(z - 2, 0)
    heads = None
    for j in range(4):
        load_p[j].wait()
        if j == 2:
            load_k = load(kc_hbm.at[0], kc)
            load_v = load(vc_hbm.at[0], vc)
            load_o = load(wo_hbm, wo)
            load_g = load(wg_hbm, wg)
            load_u = load(wu_hbm, wu)
            load_d = load(wd_hbm, wd)
        k_rows = slice(896 * j, 896 * j + 896)
        more = jnp.dot(normed[:, k_rows], wp[k_rows, :], preferred_element_type=f32)
        heads = more if heads is None else heads + more
    for j in range(4):
        proj = heads[:, HD * j : HD * j + HD].astype(bf16).astype(f32)
        a, b = proj[:, :128], proj[:, 128:]
        turned = jnp.concatenate([a * cosv - b * sinv, b * cosv + a * sinv], axis=1)
        qall[base + j] = (turned * factor).astype(bf16)
    pl.semaphore_wait(barrier, len(partners))
    for j in range(4):
        head = qall.at[base + j]
        rid = q_in + jnp.minimum(base + j, 15)
        qdst = qall.at[jnp.minimum(base + j, 15)]
        send(head, qdst, rid, at_z(2), is_query)
        send(head, qdst, rid, at_z(1 - jnp.minimum(z, 1)), is_query)
        send(head, qdst, rid, px, is_query)
        e = 4 * x + j
        send(head, fresh.at[kv], f_in + kv, (r, e), (z >= 2) & (e != s))

        @pl.when((z >= 2) & (e == s))
        def _():
            fresh[kv] = qall[base + j]

    for j in range(4):
        for a in range(2):
            h = 8 * a + 4 * x + j
            arrive(qall.at[h], q_in + h, z != a)
            send(qall.at[h], qall.at[h], q_in + h, at_z(3), z == 2)
            send(qall.at[h], qall.at[h], q_in + h, px, z != a)

    row_slot = (lax.broadcasted_iota(jnp.int32, (96, 1), 0) % 48) // STEPS
    owned = owner_ref[...] == row_slot
    eye = lax.broadcasted_iota(jnp.int32, (96, 128), 0) == lax.broadcasted_iota(jnp.int32, (96, 128), 1)
    table_row = lax.broadcasted_iota(jnp.int32, (8, 128), 0)
    table = jnp.zeros((8, 128), f32)
    bx_in = slots(4)
    load_k.wait()
    load_v.wait()
    for column in range(2):
        cx = x if column == 0 else 1 - x
        if column == 1:
            for j in range(4):
                for a in range(2):
                    h = 8 * a + 4 * cx + j
                    arrive(qall.at[h], q_in + h)
        for away in range(2):
            jj = 1 - x if away == 0 else x
            for a in range(2):
                e = 4 * a + 2 * cx + jj
                zd = e // 2
                lanes = pl.ds(pl.multiple_of(e * HD, HD), HD)
                qe = qall[pl.ds(2 * e, 2)].reshape(96, HD)
                scores = lax.dot_general(qe, kc[:, lanes], (((1,), (1,)), ((), ())), preferred_element_type=f32)
                w = jnp.where(owned, capped_weight(scores), 0.0)
                total = jnp.sum(w, axis=-1, keepdims=True)
                line = jnp.sum(jnp.where(eye, total, 0.0), axis=0, keepdims=True)
                table = jnp.where(table_row == e, line, table)
                o = jnp.dot(w.astype(bf16), vc[:, lanes], preferred_element_type=f32)
                if away == 0:
                    obuf[zd] = o.astype(bf16)
                    send(obuf.at[zd], recv_bx.at[zd], bx_in + zd, px)
                else:
                    keep_b[zd] = o
    t_in = slots(8)
    send_t[...] = table
    for k in (7, 6, 5, 4, 3, 2, 1):
        send(send_t, recv_t.at[s], t_in + s, (r, (s + k) % 8))

    bz_in = slots(4)
    for first in (1 - x, x):
        for a in range(2):
            zd = 2 * a + first
            arrive(recv_bx.at[zd], bx_in + zd)
            v = keep_b[zd] + recv_bx[zd].astype(f32)

            @pl.when(zd == z)
            def _():
                own_b[...] = v

            @pl.when(zd != z)
            def _():
                send_bz[zd] = v.astype(bf16)

            send(send_bz.at[zd], recv_bz.at[z], bz_in + z, at_z(zd), zd != z)

    arrive(fresh.at[0], f_in, 4 + s // 4 != s)
    arrive(fresh.at[1], f_in + 1, 6 + s // 4 != s)
    qe = qall[pl.ds(2 * s, 2)].reshape(96, HD)
    scores = lax.dot_general(qe, fresh[0], (((1,), (1,)), ((), ())), preferred_element_type=f32)
    ri = lax.broadcasted_iota(jnp.int32, (96, 48), 0) % 48
    ci = lax.broadcasted_iota(jnp.int32, (96, 48), 1)
    seen = (ri // STEPS == ci // STEPS) & (ci % STEPS <= ri % STEPS)
    w = jnp.where(seen, capped_weight(scores), 0.0)
    totals = jnp.sum(w, axis=-1, keepdims=True)
    fresh_out = jnp.dot(w.astype(bf16), fresh[1], preferred_element_type=f32)

    for k in range(1, 8):
        src = (s + k) % 8
        arrive(recv_t.at[src], t_in + src)
        table = table + recv_t[src]
    line = jnp.sum(jnp.where(table_row == s, table, 0.0), axis=0, keepdims=True)
    totals = totals + jnp.sum(jnp.where(eye, line, 0.0), axis=-1, keepdims=True)
    outs = fresh_out + own_b[...]
    for k in range(1, 4):
        src = (z + k) % 4
        arrive(recv_bz.at[src], bz_in + src)
        outs = outs + recv_bz[src].astype(f32)
    attended = outs / totals
    attended = jnp.concatenate([attended[:48], attended[48:]], axis=1).astype(bf16)

    z0 = (x + c) % 2
    k_me = z - z0
    is_owner = (k_me >= 0) & (k_me <= 2)
    cx_in, cz_in = slots(2), slots(8)
    load_o.wait()
    for h in range(2):
        for q in (2 * h, 2 * h + 1):
            mix32[q] = jnp.dot(attended, wo[:, 896 * q : 896 * q + 896], preferred_element_type=f32)

        def tile(k, col):
            rows = pl.ds(pl.multiple_of(24 * col + 8 * k, 8), 8)
            return mix32[2 * h, rows, :], mix32[2 * h + 1, rows, :]

        for k in range(3):
            send_cx[h, k] = pack(*tile(k, 1 - x))
        send(send_cx.at[h], recv_cx.at[h], cx_in + h, px)
    for h in range(2):
        arrive(recv_cx.at[h], cx_in + h)
        for k in range(3):
            rows = pl.ds(pl.multiple_of(24 * x + 8 * k, 8), 8)
            v = jnp.concatenate([mix32[2 * h, rows, :], mix32[2 * h + 1, rows, :]], axis=0)
            v = v + recv_cx[h, k].astype(f32)

            @pl.when(z0 + k == z)
            def _():
                own_c[h] = v

            @pl.when(z0 + k != z)
            def _():
                send_cz[h, k] = v.astype(bf16)

            send(send_cz.at[h, k], recv_cz.at[h, z], cz_in + 4 * h + z, at_z(z0 + k), z0 + k != z)

    my_rows = pl.ds(pl.multiple_of(24 * x + 8 * jnp.clip(k_me, 0, 2), 8), 8)
    k_own = jnp.clip(k_me, 0, 2)
    here = 2 * y + x

    def quarters(buf, recv, rid):
        out = []
        for h in range(2):
            v = buf[h]
            for k in range(1, 4):
                src = (z + k) % 4
                arrive(recv.at[h, src], rid + 4 * h + src)
                v = v + recv[h, src].astype(f32)
            out += [v[:8], v[8:]]
        return out

    def mean_scale(parts):
        square = sum(jnp.sum(p * p, axis=-1, keepdims=True) for p in parts)
        return lax.rsqrt(square * (1.0 / 3584.0) + epsilon)

    def cols(q):
        return slice(896 * q, 896 * q + 896)

    @pl.when(is_owner)
    def _():
        mixed = quarters(own_c, recv_cz, cz_in)
        scale = mean_scale(mixed)
        middle = [rows32[my_rows, cols(q)] + mixed[q] * scale * g2_ref[cols(q)][None, :] for q in range(4)]
        scale = mean_scale(middle)
        for q in range(4):
            mid[q] = middle[q]
        feed = [middle[q] * scale * g3_ref[cols(q)][None, :] for q in range(4)]
        for h in range(2):
            fbuf[k_own, c, here, h] = pack(feed[2 * h], feed[2 * h + 1])

    fb_in, fc_in = slots(12), slots(3)
    d0_in, d1_in, d3_in, rb_in = slots(6), slots(12), slots(4), slots(6)
    corner = ((1 - y) * 2 + c, z * 2 + 1 - x)
    beside_at, across_at, corner_at = 2 * y + 1 - x, 2 * (1 - y) + x, 2 * (1 - y) + 1 - x

    def fsend(k, dev, cond=None):
        block = fbuf.at[k, c, here]
        send(block, block, fb_in + 4 * k + here, dev, cond)

    def farrive(k, place, cond=None):
        arrive(fbuf.at[k, c, place], fb_in + 4 * k + place, cond)

    for far in (1, 2, 3):
        fsend(k_own, at_z((z + far) % 4), is_owner)

    def feed_near(k):
        farrive(k, here, z0 + k != z)
        for dev in (corner, px, py):
            fsend(k, dev)

    def feed_core(k):
        for place in (beside_at, across_at, corner_at):
            farrive(k, place)
        blocks = fbuf.at[k, c]
        send(blocks, blocks, fc_in + k, pc)

    def feed_forward(ks):
        if ks[0] == 0:
            load_g.wait()
            load_u.wait()
            load_d.wait()
        rows = slice(64 * ks[0], 64 * ks[-1] + 64)
        gate = up = None
        for h in range(2):
            for k in ks:
                if h == 0:
                    arrive(fbuf.at[k, 1 - c], fc_in + k)
                for p in range(4):
                    one, two = (fbuf[k, p // 2, 2 * (p % 2) + i, h].astype(f32) for i in range(2))
                    at = slice(64 * k + 16 * p, 64 * k + 16 * p + 16)
                    xq[0, at, :] = pack(one[:8], two[:8])
                    xq[1, at, :] = pack(one[8:], two[8:])
            for i in range(2):
                k_cols = cols(2 * h + i)
                gate_more = lax.dot_general(xq[i, rows, :], wg[:, k_cols], (((1,), (1,)), ((), ())), preferred_element_type=f32)
                up_more = lax.dot_general(xq[i, rows, :], wu[:, k_cols], (((1,), (1,)), ((), ())), preferred_element_type=f32)
                gate = gate_more if gate is None else gate + gate_more
                up = up_more if up is None else up + up_more
        bent = 0.5 * gate * (1.0 + jnp.tanh(math.sqrt(2.0 / math.pi) * (gate + 0.044715 * (gate * gate * gate))))
        hidden = (bent * up).astype(bf16)
        for h in range(2):
            for q in (2 * h, 2 * h + 1):
                part[q, rows, :] = jnp.dot(hidden, wd[:, cols(q)], preferred_element_type=f32)
            for k in ks:
                for place in range(4):
                    send_d0[h, k, place] = piece(h, k, 1 - c, place).astype(bf16)
                send(send_d0.at[h, k], recv_d0.at[h, k], d0_in + 3 * h + k, pc)

    def piece(h, k, core, place):
        rows = pl.ds(pl.multiple_of(64 * k + 32 * core + 8 * place, 8), 8)
        return jnp.concatenate([part[2 * h, rows, :], part[2 * h + 1, rows, :]], axis=0)

    def sum_core(k):
        for h in range(2):
            arrive(recv_d0.at[h, k], d0_in + 3 * h + k)
        for place, dev in ((corner_at, corner), (beside_at, px), (across_at, py), (here, None)):
            for h in range(2):
                v = piece(h, k, c, place) + recv_d0[h, k, place].astype(f32)
                if dev is None:
                    keep_d1[k, h] = v
                else:
                    send_d1[k, place, h] = v.astype(bf16)
            if dev is not None:
                send(send_d1.at[k, place], recv_d1.at[k, here], d1_in + 4 * k + here, dev)

    def sum_near(k):
        for place in (beside_at, across_at, corner_at):
            arrive(recv_d1.at[k, place], d1_in + 4 * k + place)
        mine = z0 + k == z
        for h in range(2):
            v = keep_d1[k, h]
            for place in (beside_at, across_at, corner_at):
                v = v + recv_d1[k, place, h].astype(f32)

            @pl.when(mine)
            def _():
                own_d[h] = v

            @pl.when(jnp.logical_not(mine))
            def _():
                send_d3[k, h] = v.astype(bf16)

        send(send_d3.at[k], recv_d3.at[z], d3_in + z, at_z(z0 + k), jnp.logical_not(mine))

    def rsend(t, dev, cond=None):
        send(rbuf.at[t], rbuf.at[t], rb_in + t, dev, cond)

    def finish(k):
        mine = z0 + k == z

        @pl.when(mine)
        def _():
            halves = [own_d[0], own_d[1]]
            for far in range(1, 4):
                src = (z + far) % 4
                arrive(recv_d3.at[src], d3_in + src)
                halves = [halves[h] + recv_d3[src, h].astype(f32) for h in range(2)]
            summed = [half[8 * i : 8 * i + 8] for half in halves for i in range(2)]
            scale = mean_scale(summed)
            res = [mid[q] + summed[q] * scale * g4_ref[cols(q)][None, :] for q in range(4)]
            for h in range(2):
                rbuf[3 * x + k, h] = pack(res[2 * h], res[2 * h + 1])

        for far in (1, 2, 3):
            rsend(3 * x + k, at_z((z + far) % 4), mine)

    def place_rows(t):
        for h in range(2):
            v = rbuf[t, h].astype(f32)
            for i in range(2):
                out_ref[2 * t, :, cols(2 * h + i)] = v[8 * i : 8 * i + 4].astype(bf16)
                out_ref[2 * t + 1, :, cols(2 * h + i)] = v[8 * i + 4 : 8 * i + 8].astype(bf16)

    def result_near(k):
        arrive(rbuf.at[3 * x + k], rb_in + 3 * x + k, z0 + k != z)
        rsend(3 * x + k, px)
        place_rows(3 * x + k)

    def result_far(k):
        arrive(rbuf.at[3 * (1 - x) + k], rb_in + 3 * (1 - x) + k)
        place_rows(3 * (1 - x) + k)

    for act, k in ((feed_near, 0), (feed_near, 1), (feed_near, 2), (feed_core, 0), (feed_core, 1), (feed_forward, (0,1,)), (feed_core, 2), (sum_core, 0), (sum_core, 1), (feed_forward, (2,)), (sum_core, 2), (sum_near, 0), (sum_near, 1), (sum_near, 2), (finish, 0), (finish, 1), (finish, 2), (result_near, 0), (result_near, 1), (result_near, 2), (result_far, 0), (result_far, 1), (result_far, 2)):
        act(k)

    for cond, copy in pending:
        when(cond, copy.wait_send)
    assert counts["send"] <= SENDS and counts["recv"] <= RECVS, counts


SENDS, RECVS, LOADS = 192, 192, 18


def grouped(
    embedded, cache_keys, cache_values, token_owner, dealing, lengths,
    project_weight, output_weight, gate_weight, up_weight, down_weight,
    gain_first, gain_second, gain_third, gain_fourth,
):
    f32, bf16 = jnp.float32, jnp.bfloat16
    width = embedded.shape[2]
    by_slot = embedded.transpose(1, 0, 2)
    gate_rows, up_rows = gate_weight.T, up_weight.T
    vmem = pl.BlockSpec(memory_space=pltpu.VMEM)
    hbm = pl.BlockSpec(memory_space=pl.ANY)
    V = pltpu.VMEM
    scratch = [
        pltpu.SMEM(dealing.shape, jnp.int32), pltpu.SMEM(lengths.shape, jnp.int32), V(token_owner.shape, jnp.int32),
        *[V(gain_first.shape, f32)] * 4, V(by_slot.shape, bf16),
        V(project_weight.shape, bf16), V(cache_keys.shape[1:], bf16), V(cache_values.shape[1:], bf16),
        V(output_weight.shape, bf16), V(gate_rows.shape, bf16), V(up_rows.shape, bf16), V(down_weight.shape, bf16),
        V((48, width), f32), V((48, width), bf16), V((20, 48, HD), bf16), V((2, 48, HD), bf16),
        V((4, 96, HD), bf16), V((4, 96, HD), f32), V((4, 96, HD), bf16), V((4, 96, HD), bf16), V((4, 96, HD), bf16), V((96, HD), f32),
        V((8, 128), f32), V((8, 8, 128), f32), V((4, 48, 896), f32),
        V((2, 3, 16, 896), bf16), V((2, 3, 16, 896), bf16), V((2, 3, 16, 896), bf16), V((2, 4, 16, 896), bf16), V((2, 16, 896), f32), V((4, 8, 896), f32),
        V((3, 2, 4, 2, 16, 896), bf16), V((2, 192, 896), bf16), V((4, 192, 896), f32),
        V((2, 3, 4, 16, 896), bf16), V((2, 3, 4, 16, 896), bf16),
        V((3, 4, 2, 16, 896), bf16), V((3, 4, 2, 16, 896), bf16), V((3, 2, 16, 896), f32),
        V((3, 2, 16, 896), bf16), V((4, 2, 16, 896), bf16), V((2, 16, 896), f32), V((6, 2, 16, 896), bf16),
        pltpu.SemaphoreType.DMA((LOADS,)), pltpu.SemaphoreType.DMA((SENDS,)), pltpu.SemaphoreType.DMA((RECVS,)),
    ]
    results = pl.pallas_call(
        group_kernel,
        out_shape=jax.ShapeDtypeStruct(by_slot.shape, bf16),
        in_specs=[hbm] * 15,
        out_specs=vmem,
        scratch_shapes=scratch,
        name="decode_layer",
        compiler_params=pltpu.CompilerParams(collective_id=0, has_side_effects=True, vmem_limit_bytes=56 * 2**20),
    )(
        dealing, lengths, token_owner, gain_first, gain_second, gain_third, gain_fourth, by_slot,
        project_weight, cache_keys, cache_values, output_weight, gate_rows, up_rows, down_weight,
    )
    return results.transpose(1, 0, 2)


def solution(mesh):
    fits = mesh.shape["req"] == 4 and mesh.shape["seq"] == 8
    return jax.shard_map(
        grouped if fits else body,
        mesh=mesh,
        in_specs=(
            P(None, "req", None),
            P("req", "seq", None),
            P("req", "seq", None),
            P("req", "seq"),
            P(),
            P(),
            P(None, "seq"),
            P("seq", None),
            P(None, ("req", "seq")),
            P(None, ("req", "seq")),
            P(("req", "seq"), None),
            P(),
            P(),
            P(),
            P(),
        ),
        out_specs=P(None, "req", None),
        check_vma=False,
    )
```
